768 devices in a mesh: pipe: 6 (over z_lo), seq: 32 (over y, z_hi, core), fsdp: 4 (over x).
Axes of the slice: x: 4, y: 8, z: 12 (z_hi: 2, z_lo: 6; z = z_hi * 6 + z_lo), core: 2. Of those that a mesh axis runs over, the one named last changes fastest.
Arguments:
- embedded: bfloat16 [4096, 2688], P('seq', 'fsdp'), may hold values from -6 to 6
- sent_forward: bfloat16 [6, 4096, 2688], P('pipe', 'seq', 'fsdp'), may hold values from -6 to 6
- stashed: bfloat16 [6, 4096, 2688], P('pipe', 'seq', 'fsdp'), may hold values from -6 to 6
- sent_backward: bfloat16 [6, 4096, 2688], P('pipe', 'seq', 'fsdp'), may hold values from -6 to 6
- loss_grad: bfloat16 [4096, 2688], P('seq', 'fsdp'), may hold values from -6 to 6
- norm_gain: float32 [6, 2688], P('pipe'), may hold values from 0.5 to 2
- w_query: bfloat16 [6, 2688, 2048], P('pipe', None, 'fsdp'), may hold values from -1 to 1
- w_key: bfloat16 [6, 2688, 1024], P('pipe', None, 'fsdp'), may hold values from -1 to 1
- value_projection: bfloat16 [6, 2688, 1024], P('pipe', None, 'fsdp'), may hold values from -0.125 to 0.125
- w_out: bfloat16 [6, 2048, 2688], P('pipe', 'fsdp'), may hold values from -0.125 to 0.125
- forward_docs: int32 [6, 4096], P('pipe'), may hold values from 0 to 3, never falling along the last dimension, each value on 1 to 2048 neighbouring positions
- backward_docs: int32 [6, 4096], P('pipe'), may hold values from 0 to 3, never falling along the last dimension, each value on 1 to 2048 neighbouring positions
Outputs:
- forward_out: bfloat16 [6, 4096, 2688], P('pipe', 'seq', 'fsdp')
- input_grad: bfloat16 [6, 4096, 2688], P('pipe', 'seq', 'fsdp')
The draws below stay inside these ranges and needn't reach their ends.
Inputs may be any that keep to these rules, and one draw needn't show every extreme that they name: `forward_docs`: document numbers never fall along a sequence; every document is a run of 1 to 2048 tokens. `backward_docs`: document numbers never fall along a sequence; every document is a run of 1 to 2048 tokens.
All inputs are finite; a program needn't handle non-finite values.
Results may differ from the reference program's by a relative error of at most 0.015.
Values may be sent and summed in bfloat16 or wider, within the bound.
No kernel may reach another device: no remote copies, remote signals or barrier semaphores. Data moves between devices by JAX's collectives and lax.ppermute only.
A program may use at most 64 MiB of HBM per device.

```python
import math
import jax
import jax.numpy as jnp
import numpy as np
from jax import lax

MODEL_WIDTH = 2688
QUERY_HEADS = 16
KEY_VALUE_HEADS = 8
HEAD_SIZE = 128
WINDOW_TOKENS = 512
SHARD_TOKENS = 128
SEQUENCE_TOKENS = 4096
N_PIPE = 6
N_SEQ = 32


def plant_pattern(key):
    pattern_random_key = jax.random.fold_in(key, 9173)
    head_sign_flips = (jax.random.randint(jax.random.fold_in(pattern_random_key, 3), (KEY_VALUE_HEADS, HEAD_SIZE), 0, 2) * 2 - 1).astype(jnp.float32)
    return head_sign_flips


def draw_rows(key, leading, salt):
    own_key = jax.random.fold_in(key, salt)
    full_shape = leading + (SEQUENCE_TOKENS, MODEL_WIDTH)
    drawn = jax.random.truncated_normal(own_key, -6.0, 6.0, full_shape, jnp.float32)
    return drawn.astype(jnp.bfloat16)


def draw_projection(key, aligned_rows, salt):
    own_key = jax.random.fold_in(key, salt)
    columns = aligned_rows.shape[0]
    spread = MODEL_WIDTH ** (-0.5)
    full_shape = (N_PIPE, MODEL_WIDTH, columns)
    drawn = jax.random.truncated_normal(own_key, -6.0, 6.0, full_shape, jnp.float32) * spread
    return drawn.astype(jnp.bfloat16)


def draw_embedded(key, part):
    return draw_rows(key, (), 11)


def draw_sent_forward(key, part):
    return draw_rows(key, (N_PIPE,), 12)


def draw_stashed(key, part):
    return draw_rows(key, (N_PIPE,), 13)


def draw_w_query(key, part):
    head_sign_flips = plant_pattern(key)
    aligned_rows = jnp.repeat(head_sign_flips, QUERY_HEADS // KEY_VALUE_HEADS, axis=0).reshape(QUERY_HEADS * HEAD_SIZE)
    return draw_projection(key, aligned_rows, 21)


def draw_w_key(key, part):
    head_sign_flips = plant_pattern(key)
    aligned_rows = head_sign_flips.reshape(KEY_VALUE_HEADS * HEAD_SIZE)
    return draw_projection(key, aligned_rows, 22)


def levels(rng, shape, shards, least, high):
    level = 1.0
    for dim, shards_of in shards:
        draws = jax.random.uniform(jax.random.fold_in(jax.random.fold_in(rng, 6), dim), (shards_of,), jnp.float32, least / len(shards), high / len(shards))
        level = level * jnp.repeat(jnp.exp(draws), shape[dim] // shards_of).reshape((-1,) + (1,) * (len(shape) - 1 - dim))
    return level


def split_up(number_of, total, bound, skew):
    loads = [(1 << 20) // math.isqrt(standing ** skew) + 1 for standing in range(2, number_of + 1)]
    rest, given = total - bound - (number_of - 1), [1] * (number_of - 1)
    while rest > 0:
        free = [i for i in range(number_of - 1) if given[i] < bound]
        whole, budget = sum([loads[i] for i in free]), rest
        for i in free:
            extra = min(bound - given[i], max(1, budget * loads[i] // whole), rest)
            given[i] = given[i] + extra
            rest = rest - extra
    return np.array([bound] + given)


def ragged(key, amount, total, limit, lean):
    if amount == 2:
        one = jax.random.randint(key, (), max(1, total - limit), min(limit, total - 1) + 1)
        return jnp.stack([one, total - one])
    lengths = jnp.asarray(split_up(amount, total, limit, lean), jnp.int32)
    couples = (amount - 1) // 2
    source_of, receiver = lengths[1:1 + 2 * couples:2], lengths[2:2 + 2 * couples:2]
    margin = jnp.minimum(source_of - 1, limit - receiver)
    moved = jax.random.randint(jax.random.fold_in(key, 1), (couples,), 0, 1 << 20) % (margin + 1)
    lengths = lengths.at[1:1 + 2 * couples:2].set(source_of - moved).at[2:2 + 2 * couples:2].set(receiver + moved)
    return lengths[jax.random.permutation(jax.random.fold_in(key, 2), amount)]


def normal_values(key, extent, scale, limit, split=(), held_as=jnp.bfloat16):
    loudness = levels(key, extent, split, -0.22, 0.18) if split else 1.0
    array = jax.random.normal(key, extent, jnp.float32) * scale * loudness
    return jnp.minimum(jnp.maximum(array, -limit), limit).astype(held_as)


def setup_inputs(seed: int = 0) -> dict:
    key_list = jax.random.split(jax.random.key(seed), 13)
    return {
        "embedded": draw_embedded(jax.random.fold_in(key_list[12], 71), 0),
        "sent_forward": draw_sent_forward(jax.random.fold_in(key_list[12], 71), 0),
        "stashed": draw_stashed(jax.random.fold_in(key_list[12], 71), 0),
        "sent_backward": normal_values(key_list[3], (N_PIPE, SEQUENCE_TOKENS, MODEL_WIDTH), 1.0, 6.0, ((0, 6), (1, 32), (2, 4))),
        "loss_grad": normal_values(key_list[4], (SEQUENCE_TOKENS, MODEL_WIDTH), 1.0, 6.0, ((0, 32), (1, 4))),
        "norm_gain": jnp.clip(jnp.exp(math.log(2.0) - 1.3862944 * jax.random.uniform(key_list[5], (N_PIPE, MODEL_WIDTH), jnp.float32) ** levels(key_list[5], (N_PIPE, MODEL_WIDTH), ((0, 6),), -0.2, 0.2)), 0.5, 2.0),
        "w_query": draw_w_query(jax.random.fold_in(key_list[12], 71), 0),
        "w_key": draw_w_key(jax.random.fold_in(key_list[12], 71), 0),
        "value_projection": normal_values(key_list[8], (N_PIPE, MODEL_WIDTH, KEY_VALUE_HEADS * HEAD_SIZE), MODEL_WIDTH ** -0.5, 0.125, ((0, 6), (2, 4))),
        "w_out": normal_values(key_list[9], (N_PIPE, QUERY_HEADS * HEAD_SIZE, MODEL_WIDTH), (QUERY_HEADS * HEAD_SIZE) ** -0.5, 0.125, ((0, 6), (1, 4))),
        "forward_docs": jax.vmap(lambda own: jnp.searchsorted(jnp.cumsum(ragged(own, 4, SEQUENCE_TOKENS, SEQUENCE_TOKENS // 2, 1)), jnp.arange(SEQUENCE_TOKENS), side="right"))(jax.random.split(key_list[10], N_PIPE)).reshape((N_PIPE, SEQUENCE_TOKENS)).astype(jnp.int32),
        "backward_docs": jax.vmap(lambda own: jnp.searchsorted(jnp.cumsum(ragged(own, 4, SEQUENCE_TOKENS, SEQUENCE_TOKENS // 2, 1)), jnp.arange(SEQUENCE_TOKENS), side="right"))(jax.random.split(key_list[11], N_PIPE)).reshape((N_PIPE, SEQUENCE_TOKENS)).astype(jnp.int32),
    }


def normalize(rows_in, gain):
    value_rows = rows_in.astype(jnp.float32)
    row_scale_factor = lax.rsqrt(lax.optimization_barrier(jnp.mean(value_rows * value_rows, axis=-1, keepdims=True)) + 1e-06)
    return ((value_rows * row_scale_factor * gain).astype(jnp.bfloat16), row_scale_factor)

def padded_docs(docs):
    return jnp.concatenate([jnp.full((WINDOW_TOKENS,), -1, jnp.int32), docs.astype(jnp.int32)])

def block_probs(query_block, k_block, q_pos, k_pos, q_doc, k_doc):
    scores = jnp.einsum('qhgd,khd->hgqk', query_block.astype(jnp.float32), k_block.astype(jnp.float32))
    scores = scores * HEAD_SIZE ** (-0.5)
    keep = (k_pos[None, :] <= q_pos[:, None]) & (q_pos[:, None] - k_pos[None, :] < WINDOW_TOKENS)
    keep = keep & (k_doc[None, :] == q_doc[:, None])
    scores = jnp.where(keep, scores, -1e+30)
    top = lax.optimization_barrier(jnp.max(scores, axis=-1, keepdims=True))
    expo = jnp.exp(scores - top)
    return expo / lax.optimization_barrier(jnp.sum(expo, axis=-1, keepdims=True))

def project(x_rows, gain, wq, wk, wv):
    h_rows, row_scale_factor = normalize(x_rows, gain)
    query_rows = jnp.dot(h_rows, wq, preferred_element_type=jnp.float32).astype(jnp.bfloat16)
    key_rows = jnp.dot(h_rows, wk, preferred_element_type=jnp.float32).astype(jnp.bfloat16)
    value_rows = jnp.dot(h_rows, wv, preferred_element_type=jnp.float32).astype(jnp.bfloat16)
    return (query_rows, key_rows.reshape(SEQUENCE_TOKENS, KEY_VALUE_HEADS, HEAD_SIZE), value_rows.reshape(SEQUENCE_TOKENS, KEY_VALUE_HEADS, HEAD_SIZE), row_scale_factor)

def block_inputs(query_rows, key_pad, value_pad, doc_pad, index):
    head_groups = QUERY_HEADS // KEY_VALUE_HEADS
    query_start = (index * SHARD_TOKENS).astype(jnp.int32)
    query_block = lax.dynamic_slice_in_dim(query_rows, query_start, SHARD_TOKENS, 0).reshape(SHARD_TOKENS, KEY_VALUE_HEADS, head_groups, HEAD_SIZE)
    k_block = lax.dynamic_slice_in_dim(key_pad, query_start, WINDOW_TOKENS + SHARD_TOKENS, 0)
    v_block = lax.dynamic_slice_in_dim(value_pad, query_start, WINDOW_TOKENS + SHARD_TOKENS, 0)
    q_pos = query_start + jnp.arange(SHARD_TOKENS, dtype=jnp.int32)
    k_pos = query_start - WINDOW_TOKENS + jnp.arange(WINDOW_TOKENS + SHARD_TOKENS, dtype=jnp.int32)
    q_doc = lax.dynamic_slice_in_dim(doc_pad, query_start + WINDOW_TOKENS, SHARD_TOKENS, 0)
    k_doc = lax.dynamic_slice_in_dim(doc_pad, query_start, WINDOW_TOKENS + SHARD_TOKENS, 0)
    return (query_block, k_block, v_block, q_pos, k_pos, q_doc, k_doc)

def pad_rows(block):
    return jnp.concatenate([jnp.zeros((WINDOW_TOKENS,) + block.shape[1:], block.dtype), block], 0)

def layer_forward(x_rows, gain, wq, wk, wv, wo, docs):
    query_rows, key_rows, value_rows, row_scale_factor = project(x_rows, gain, wq, wk, wv)
    key_pad, value_pad, doc_pad = (pad_rows(key_rows), pad_rows(value_rows), padded_docs(docs))

    def one_block(index):
        query_block, k_block, v_block, q_pos, k_pos, q_doc, k_doc = block_inputs(query_rows, key_pad, value_pad, doc_pad, index)
        probs = block_probs(query_block, k_block, q_pos, k_pos, q_doc, k_doc).astype(jnp.bfloat16)
        attn = jnp.einsum('hgqk,khd->qhgd', probs.astype(jnp.float32), v_block.astype(jnp.float32))
        return attn.reshape(SHARD_TOKENS, QUERY_HEADS * HEAD_SIZE).astype(jnp.bfloat16)
    attn_all = lax.map(one_block, jnp.arange(N_SEQ, dtype=jnp.int32)).reshape(SEQUENCE_TOKENS, QUERY_HEADS * HEAD_SIZE)
    mixed = jnp.dot(attn_all, wo, preferred_element_type=jnp.float32)
    return (x_rows.astype(jnp.float32) + mixed).astype(jnp.bfloat16)

def layer_backward(x_rows, upstream, gain, wq, wk, wv, wo, docs):
    query_rows, key_rows, value_rows, row_scale_factor = project(x_rows, gain, wq, wk, wv)
    key_pad, value_pad, doc_pad = (pad_rows(key_rows), pad_rows(value_rows), padded_docs(docs))
    attention_gradient = jnp.dot(upstream, wo.T, preferred_element_type=jnp.float32).astype(jnp.bfloat16)

    def one_block(carry, index):
        key_gradient_padded, value_gradient_padded = carry
        query_block, k_block, v_block, q_pos, k_pos, q_doc, k_doc = block_inputs(query_rows, key_pad, value_pad, doc_pad, index)
        probs = block_probs(query_block, k_block, q_pos, k_pos, q_doc, k_doc)
        probs_low = probs.astype(jnp.bfloat16).astype(jnp.float32)
        query_start = (index * SHARD_TOKENS).astype(jnp.int32)
        attention_block_gradient = lax.dynamic_slice_in_dim(attention_gradient, query_start, SHARD_TOKENS, 0).reshape(SHARD_TOKENS, KEY_VALUE_HEADS, QUERY_HEADS // KEY_VALUE_HEADS, HEAD_SIZE).astype(jnp.float32)
        dv_block = jnp.einsum('hgqk,qhgd->khd', probs_low, attention_block_gradient)
        dp_block = jnp.einsum('qhgd,khd->hgqk', attention_block_gradient, v_block.astype(jnp.float32))
        delta = lax.optimization_barrier(jnp.sum(probs * dp_block, axis=-1, keepdims=True))
        ds_block = (probs * (dp_block - delta)).astype(jnp.bfloat16).astype(jnp.float32)
        dq_block = jnp.einsum('hgqk,khd->qhgd', ds_block, k_block.astype(jnp.float32)) * HEAD_SIZE ** (-0.5)
        dk_block = jnp.einsum('hgqk,qhgd->khd', ds_block, query_block.astype(jnp.float32)) * HEAD_SIZE ** (-0.5)
        old_k = lax.dynamic_slice_in_dim(key_gradient_padded, query_start, WINDOW_TOKENS + SHARD_TOKENS, 0)
        old_v = lax.dynamic_slice_in_dim(value_gradient_padded, query_start, WINDOW_TOKENS + SHARD_TOKENS, 0)
        key_gradient_padded = lax.dynamic_update_slice_in_dim(key_gradient_padded, old_k + dk_block, query_start, 0)
        value_gradient_padded = lax.dynamic_update_slice_in_dim(value_gradient_padded, old_v + dv_block, query_start, 0)
        return ((key_gradient_padded, value_gradient_padded), dq_block.reshape(SHARD_TOKENS, QUERY_HEADS * HEAD_SIZE).astype(jnp.bfloat16))
    padded_start = jnp.zeros((WINDOW_TOKENS + SEQUENCE_TOKENS, KEY_VALUE_HEADS, HEAD_SIZE), jnp.float32)
    (key_gradient_padded, value_gradient_padded), dq_all = lax.scan(one_block, (padded_start, padded_start), jnp.arange(N_SEQ, dtype=jnp.int32))
    dq_all = dq_all.reshape(SEQUENCE_TOKENS, QUERY_HEADS * HEAD_SIZE)
    key_gradient_total = key_gradient_padded[WINDOW_TOKENS:].reshape(SEQUENCE_TOKENS, KEY_VALUE_HEADS * HEAD_SIZE).astype(jnp.bfloat16)
    value_gradient_total = value_gradient_padded[WINDOW_TOKENS:].reshape(SEQUENCE_TOKENS, KEY_VALUE_HEADS * HEAD_SIZE).astype(jnp.bfloat16)
    d_norm = jnp.dot(dq_all, wq.T, preferred_element_type=jnp.float32)
    d_norm = d_norm + jnp.dot(key_gradient_total, wk.T, preferred_element_type=jnp.float32)
    d_norm = d_norm + jnp.dot(value_gradient_total, wv.T, preferred_element_type=jnp.float32)
    values_in = x_rows.astype(jnp.float32)
    row_mean = lax.optimization_barrier(jnp.mean(values_in * gain * d_norm, axis=-1, keepdims=True))
    d_input = row_scale_factor * gain * d_norm - values_in * row_scale_factor ** 3 * row_mean
    return (upstream.astype(jnp.float32) + d_input).astype(jnp.bfloat16)

def reference(embedded, sent_forward, stashed, sent_backward, loss_grad, norm_gain, w_query, w_key, value_projection, w_out, forward_docs, backward_docs):
    outputs = []
    gradients = []
    for section in range(N_PIPE):
        x_rows = embedded if section == 0 else sent_forward[section - 1]
        upstream = loss_grad if section == N_PIPE - 1 else sent_backward[section + 1]
        outputs.append(layer_forward(x_rows, norm_gain[section], w_query[section], w_key[section], value_projection[section], w_out[section], forward_docs[section]))
        gradients.append(layer_backward(stashed[section], upstream, norm_gain[section], w_query[section], w_key[section], value_projection[section], w_out[section], backward_docs[section]))
    return (jnp.stack(outputs), jnp.stack(gradients))
```

```python
import jax
import jax.numpy as jnp
from jax import lax
from jax.experimental import pallas as pl
from jax.experimental.pallas import tpu as pltpu
from jax.sharding import PartitionSpec as P

HEAD = 128
WINDOW = 512
SCALE = HEAD ** (-0.5)
BF = jnp.bfloat16
F32 = jnp.float32


def dot_nn(left, right):
    return lax.dot_general(left, right, (((1,), (0,)), ((), ())), preferred_element_type=F32)


def dot_nt(left, right):
    return lax.dot_general(left, right, (((1,), (1,)), ((), ())), preferred_element_type=F32)


def dot_tn(left, right):
    return lax.dot_general(left, right, (((0,), (0,)), ((), ())), preferred_element_type=F32)


def vmem(count):
    return [pl.BlockSpec(memory_space=pltpu.VMEM) for _ in range(count)]


def smem():
    return pl.BlockSpec(memory_space=pltpu.SMEM)


def project_rows(rows, gain_ref, wq_ref, wk_ref, wv_ref, q_ref, kv_ref):
    parts = len(rows)
    width = parts * rows[0].shape[1]
    total = sum(jnp.sum(row * row, axis=1, keepdims=True) for row in rows)
    factor = lax.rsqrt(total / width + 1e-06)
    query = key = value = 0.0
    for part in range(parts):
        h = (rows[part] * factor * gain_ref[part]).astype(BF)
        query = query + dot_nn(h, wq_ref[part])
        key = key + dot_nn(h, wk_ref[part])
        value = value + dot_nn(h, wv_ref[part])
    q_ref[...] = query.astype(BF)
    half = kv_ref.shape[1] // 2
    kv_ref[:, :half] = key.astype(BF)
    kv_ref[:, half:] = value.astype(BF)
    return factor


def project_back_body(x_ref, gain_ref, wq_ref, wk_ref, wv_ref, q_ref, kv_ref, r_ref):
    rows = [x_ref[part].astype(F32) for part in range(x_ref.shape[0])]
    factor = project_rows(rows, gain_ref, wq_ref, wk_ref, wv_ref, q_ref, kv_ref)
    r_ref[...] = jnp.broadcast_to(factor, r_ref.shape)


def project_front_body(x_ref, gain_ref, wq_ref, wk_ref, wv_ref, wo_ref, q_ref, kv_ref, da_ref):
    length = q_ref.shape[0]
    parts, _, share = x_ref.shape
    rows = [x_ref[part, :length, :].astype(F32) for part in range(parts)]
    project_rows(rows, gain_ref, wq_ref, wk_ref, wv_ref, q_ref, kv_ref)
    grad = 0.0
    for part in range(parts):
        weight = wo_ref[:, part * share : (part + 1) * share]
        grad = grad + dot_nt(x_ref[part, length:, :], weight)
    da_ref[...] = grad.astype(BF)


def window_mask(info_ref, docs_ref, length):
    core = info_ref[0]
    index = info_ref[1]
    offsets = (0, 2, 4, 3 - 2 * core, 1 + 2 * core)
    q_row = jnp.broadcast_to(docs_ref[pl.ds(index, 1), :], (length, length))
    q_doc = jnp.transpose(q_row)
    across = lax.broadcasted_iota(jnp.int32, (length, length), 1)
    down = lax.broadcasted_iota(jnp.int32, (length, length), 0)
    masks = []
    for offset in offsets:
        block = index - offset
        k_doc = docs_ref[pl.ds(jnp.maximum(block, 0), 1), :]
        ahead = down - across + offset * length
        keep = (ahead >= 0) & (ahead < WINDOW) & (block >= 0)
        masks.append(keep & (jnp.broadcast_to(k_doc, (length, length)) == q_doc))
    return jnp.concatenate([jnp.where(m, 0.0, -1e30) for m in masks], axis=1)


def softmax_rows(q_rows, keys, bias):
    scores = dot_nt(q_rows, keys) * SCALE + bias
    top = jnp.max(scores, axis=1, keepdims=True)
    expo = jnp.exp(scores - top)
    return expo / jnp.sum(expo, axis=1, keepdims=True)


def attend_body(info_ref, docs_ref, q_ref, own, two, four, late, mid, wo_ref, out_ref):
    length = q_ref.shape[0]
    parts, _, share = out_ref.shape
    kv_heads = own.shape[1] // (2 * HEAD)
    groups = q_ref.shape[1] // HEAD // kv_heads
    bias = window_mask(info_ref, docs_ref, length)
    blocks = (own, two, four, mid, late)
    heads = []
    for kv in range(kv_heads):
        keys = jnp.concatenate([b[:, kv * HEAD : (kv + 1) * HEAD] for b in blocks], axis=0)
        at = (kv_heads + kv) * HEAD
        values = jnp.concatenate([b[:, at : at + HEAD] for b in blocks], axis=0)
        for group in range(groups):
            head = kv * groups + group
            rows = q_ref[:, head * HEAD : (head + 1) * HEAD]
            probs = softmax_rows(rows, keys, bias).astype(BF)
            heads.append(dot_nn(probs, values).astype(BF))
    mixed = jnp.concatenate(heads, axis=1)
    for part in range(parts):
        weight = wo_ref[:, part * share : (part + 1) * share]
        out_ref[part] = dot_nn(mixed, weight).astype(BF)


def attend_back_body(
    info_ref, docs_ref, q_ref, da_ref, own, two, four, late, mid,
    dq_ref, town_ref, ttwo_ref, tfour_ref, tswap_ref,
):
    length = q_ref.shape[0]
    kv_heads = own.shape[1] // (2 * HEAD)
    groups = q_ref.shape[1] // HEAD // kv_heads
    bias = window_mask(info_ref, docs_ref, length)
    blocks = (own, two, four, mid, late)
    for kv in range(kv_heads):
        keys = jnp.concatenate([b[:, kv * HEAD : (kv + 1) * HEAD] for b in blocks], axis=0)
        at = (kv_heads + kv) * HEAD
        values = jnp.concatenate([b[:, at : at + HEAD] for b in blocks], axis=0)
        d_key = d_value = 0.0
        for group in range(groups):
            head = kv * groups + group
            span = slice(head * HEAD, (head + 1) * HEAD)
            rows = q_ref[:, span]
            grad = da_ref[:, span]
            probs = softmax_rows(rows, keys, bias)
            d_value = d_value + dot_tn(probs.astype(BF), grad)
            d_probs = dot_nt(grad, values)
            delta = jnp.sum(probs * d_probs, axis=1, keepdims=True)
            d_scores = (probs * (d_probs - delta)).astype(BF)
            dq_ref[:, span] = (dot_nn(d_scores, keys) * SCALE).astype(BF)
            d_key = d_key + dot_tn(d_scores, rows)
        for terms, start in ((d_key, kv * HEAD), (d_value, at)):
            cols = slice(start, start + HEAD)
            town_ref[:, cols] = terms[:length]
            ttwo_ref[:, cols] = terms[length : 2 * length]
            tfour_ref[:, cols] = terms[2 * length : 3 * length]
            tswap_ref[:length, cols] = terms[4 * length :].astype(BF)
            tswap_ref[length:, cols] = terms[3 * length : 4 * length].astype(BF)


def input_terms_body(
    dq_ref, own_ref, two_ref, four_ref, x_ref, gain_ref, wq_ref, wk_ref, wv_ref, out_ref
):
    parts, _, share = x_ref.shape
    half = own_ref.shape[1] // 2
    total = own_ref[...] + two_ref[...].astype(F32) + four_ref[...].astype(F32)
    d_key = (total[:, :half] * SCALE).astype(BF)
    d_value = total[:, half:].astype(BF)
    row = 0.0
    for part in range(parts):
        d_norm = dot_nt(dq_ref[...], wq_ref[part])
        d_norm = d_norm + dot_nt(d_key, wk_ref[part])
        d_norm = d_norm + dot_nt(d_value, wv_ref[part])
        out_ref[part, :, :share] = d_norm.astype(BF)
        product = x_ref[part].astype(F32) * gain_ref[part] * d_norm
        row = row + jnp.sum(product, axis=1, keepdims=True)
    high = row.astype(BF)
    low = (row - high.astype(F32)).astype(BF)
    for part in range(parts):
        out_ref[part, :, share : share + 1] = high
        out_ref[part, :, share + 1 : share + 2] = low


def finish_body(info_ref, sums_ref, x_ref, up_ref, gain_ref, r_ref, out_ref):
    parts = sums_ref.shape[0]
    share = x_ref.shape[1]
    total = sum(sums_ref[part].astype(F32) for part in range(parts))
    row = total[:, share : share + 1] + total[:, share + 1 : share + 2]
    row = row / (parts * share)
    factor = r_ref[:, :1]
    gain = gain_ref[info_ref[2]]
    values = x_ref[...].astype(F32)
    d_input = factor * gain * total[:, :share] - values * (factor * factor * factor * row)
    out_ref[...] = (up_ref[...].astype(F32) + d_input).astype(BF)


def shifted(value, steps):
    count = lax.axis_size("seq")
    pairs = [(s, s + steps) for s in range(count) if 0 <= s + steps < count]
    return lax.ppermute(value, "seq", pairs)


def swapped(value):
    count = lax.axis_size("seq")
    return lax.ppermute(value, "seq", [(s, s ^ 1) for s in range(count)])


def next_section(value, steps):
    count = lax.axis_size("pipe")
    pairs = [(s, s + steps) for s in range(count) if 0 <= s + steps < count]
    return lax.ppermute(value, "pipe", pairs)


def gather_parts(value):
    parts = lax.axis_size("fsdp")
    spread = jnp.broadcast_to(value[None], (parts,) + value.shape)
    return lax.all_to_all(spread, "fsdp", 0, 0)


def window_blocks(kv, core):
    two = shifted(kv, 2)
    four = shifted(kv, 4)
    mid = swapped(jnp.where(core == 0, kv, four))
    late = swapped(two)
    return (kv, two, four, late, mid)


def per_device(
    embedded, sent_forward, stashed, sent_backward, loss_grad, norm_gain,
    w_query, w_key, value_projection, w_out, forward_docs, backward_docs,
):
    length, share = embedded.shape
    parts = lax.axis_size("fsdp")
    section = lax.axis_index("pipe")
    sections = lax.axis_size("pipe")
    index = lax.axis_index("seq")
    core = index % 2
    info = jnp.stack([core, index, lax.axis_index("fsdp")]).astype(jnp.int32)
    gain = norm_gain[0].reshape(parts, 1, share)
    wq = w_query[0].reshape(parts, share, -1)
    wk = w_key[0].reshape(parts, share, -1)
    wv = value_projection[0].reshape(parts, share, -1)
    wo = w_out[0]
    docs_front = forward_docs[0].reshape(-1, length)
    docs_back = backward_docs[0].reshape(-1, length)
    q_cols = wq.shape[2]
    kv_cols = 2 * wk.shape[2]
    rows_q = jax.ShapeDtypeStruct((length, q_cols), BF)
    rows_kv = jax.ShapeDtypeStruct((length, kv_cols), BF)
    terms = jax.ShapeDtypeStruct((length, kv_cols), F32)

    arrived = next_section(sent_forward[0], 1)
    returned = next_section(sent_backward[0], -1)
    stash = gather_parts(stashed[0])
    incoming = jnp.where(section == 0, embedded, arrived)
    upstream = jnp.where(section == sections - 1, loss_grad, returned)
    both = gather_parts(jnp.concatenate([incoming, upstream], 0))

    q_back, kv_back, factor = pl.pallas_call(
        project_back_body,
        out_shape=(rows_q, rows_kv, jax.ShapeDtypeStruct((length, HEAD), F32)),
        in_specs=vmem(5), out_specs=tuple(vmem(3)), name="project_back",
    )(stash, gain, wq, wk, wv)
    blocks_back = window_blocks(kv_back, core)

    q_front, kv_front, d_attn = pl.pallas_call(
        project_front_body,
        out_shape=(rows_q, rows_kv, rows_q),
        in_specs=vmem(6), out_specs=tuple(vmem(3)), name="project_front",
    )(both, gain, wq, wk, wv, wo)
    blocks_front = window_blocks(kv_front, core)

    d_query, t_own, t_two, t_four, t_swap = pl.pallas_call(
        attend_back_body,
        out_shape=(rows_q, terms, terms, terms, jax.ShapeDtypeStruct((2 * length, kv_cols), BF)),
        in_specs=[smem()] + vmem(8), out_specs=tuple(vmem(5)), name="attend_back",
    )(info, docs_back, q_back, d_attn, *blocks_back)
    t_swap = swapped(t_swap)
    t_late = t_swap[:length].astype(F32)
    t_mid = t_swap[length:].astype(F32)
    back_two = shifted((t_two + t_late).astype(BF), -2)
    back_four = shifted(jnp.where(core == 0, t_four, t_four + t_mid).astype(BF), -4)
    t_own = jnp.where(core == 0, t_own + t_mid, t_own)

    partial_out = pl.pallas_call(
        attend_body,
        out_shape=jax.ShapeDtypeStruct((parts, length, share), BF),
        in_specs=[smem()] + vmem(8), out_specs=vmem(1)[0], name="attend",
    )(info, docs_front, q_front, *blocks_front, wo)
    summed = jnp.sum(lax.all_to_all(partial_out, "fsdp", 0, 0).astype(F32), 0)
    forward_out = (incoming.astype(F32) + summed).astype(BF)

    padded = -(-(share + 2) // 128) * 128
    d_parts = pl.pallas_call(
        input_terms_body,
        out_shape=jax.ShapeDtypeStruct((parts, length, padded), BF),
        in_specs=vmem(9), out_specs=vmem(1)[0], name="input_terms",
    )(d_query, t_own, back_two, back_four, stash, gain, wq, wk, wv)
    d_parts = lax.all_to_all(d_parts, "fsdp", 0, 0)
    input_grad = pl.pallas_call(
        finish_body,
        out_shape=jax.ShapeDtypeStruct((length, share), BF),
        in_specs=[smem()] + vmem(5), out_specs=vmem(1)[0], name="finish",
    )(info, d_parts, stashed[0], upstream, gain, factor)
    return (forward_out[None], input_grad[None])


def solution(mesh):
    placed = (
        P("seq", "fsdp"),
        P("pipe", "seq", "fsdp"),
        P("pipe", "seq", "fsdp"),
        P("pipe", "seq", "fsdp"),
        P("seq", "fsdp"),
        P("pipe", None),
        P("pipe", None, "fsdp"),
        P("pipe", None, "fsdp"),
        P("pipe", None, "fsdp"),
        P("pipe", "fsdp", None),
        P("pipe", None),
        P("pipe", None),
    )
    return jax.shard_map(
        per_device,
        mesh=mesh,
        in_specs=placed,
        out_specs=(P("pipe", "seq", "fsdp"), P("pipe", "seq", "fsdp")),
        check_vma=False,
    )
```

```python
import jax
import jax.numpy as jnp
from jax import lax
from jax.experimental import pallas as pl
from jax.experimental.pallas import tpu as pltpu
from jax.sharding import PartitionSpec as P


HEAD = 128
WINDOW = 512
SCALE = HEAD ** (-0.5)
BF = jnp.bfloat16
F32 = jnp.float32
LIMIT = 14
SENDS = (0, 1, 3, 2)


def dot_nn(left, right):
    return lax.dot_general(left, right, (((1,), (0,)), ((), ())), preferred_element_type=F32)


def dot_nt(left, right):
    return lax.dot_general(left, right, (((1,), (1,)), ((), ())), preferred_element_type=F32)


def dot_tn(left, right):
    return lax.dot_general(left, right, (((0,), (0,)), ((), ())), preferred_element_type=F32)


def vmem(count):
    return [pl.BlockSpec(memory_space=pltpu.VMEM) for _ in range(count)]


def smem():
    return pl.BlockSpec(memory_space=pltpu.SMEM)


def limit(mebibytes):
    return pltpu.CompilerParams(vmem_limit_bytes=mebibytes * 2**20)


def cost(microseconds):
    return pl.CostEstimate(
        flops=0, transcendentals=0, bytes_accessed=int(microseconds * 3_300_000)
    )


def kernel(body, mebibytes, out_shape, in_specs, microseconds=4.0, scratch=()):
    single = not isinstance(out_shape, tuple)
    return pl.pallas_call(
        body,
        out_shape=out_shape,
        in_specs=in_specs,
        out_specs=vmem(1)[0] if single else tuple(vmem(len(out_shape))),
        scratch_shapes=scratch,
        compiler_params=limit(mebibytes),
        cost_estimate=cost(microseconds),
    )


def stacked(ref, start, share):
    return jnp.concatenate([ref[part, start : start + share, :] for part in range(ref.shape[0])], 0)


def normal_rows(value, gain_ref):
    value = jnp.transpose(value).astype(F32)
    mean = jnp.mean(value * value, axis=1, keepdims=True)
    factor = lax.rsqrt(mean + 1e-06)
    return (value * factor * gain_ref[...]).astype(BF), factor


def across(column):
    length = column.shape[0]
    return jnp.transpose(jnp.broadcast_to(column, (length, length)))


def project_rows(h, wk_ref, wv_ref, wq_ref, q_ref, kv_ref):
    half = kv_ref.shape[1] // 2
    kv_ref[:, :half] = dot_nn(h, wk_ref[...]).astype(BF)
    kv_ref[:, half:] = dot_nn(h, wv_ref[...]).astype(BF)
    q_ref[...] = dot_nn(h, wq_ref[...]).astype(BF)


def placed_parts(info_ref, own, one, minus, far, hold_ref):
    place = info_ref[2]
    parts = hold_ref.shape[0]
    for offset, piece in ((0, own), (parts - 1, one), (1, minus), (2, far)):
        hold_ref[lax.rem(place + offset, parts)] = piece[...]


def project_back_body(
    info_ref, own, one, minus, far, gain_ref, wk_ref, wv_ref, wq_ref,
    q_ref, kv_ref, r_ref, hold_ref,
):
    placed_parts(info_ref, own, one, minus, far, hold_ref)
    h, factor = normal_rows(stacked(hold_ref, 0, hold_ref.shape[1]), gain_ref)
    r_ref[...] = jnp.broadcast_to(factor, r_ref.shape)
    project_rows(h, wk_ref, wv_ref, wq_ref, q_ref, kv_ref)


def project_front_body(
    info_ref, own, one, minus, far, gain_ref, wk_ref, wv_ref, wq_ref, wo_ref,
    q_ref, kv_ref, da_ref, hold_ref,
):
    placed_parts(info_ref, own, one, minus, far, hold_ref)
    share = hold_ref.shape[1] // 2
    h, _ = normal_rows(stacked(hold_ref, 0, share), gain_ref)
    project_rows(h, wk_ref, wv_ref, wq_ref, q_ref, kv_ref)
    grad = dot_nn(wo_ref[...], stacked(hold_ref, share, share))
    da_ref[...] = jnp.transpose(grad.astype(BF))


def touch_body(info_ref, gain_ref, wk_ref, wv_ref, wq_ref, wo_ref, out_ref, hold_ref):
    share, length = out_ref.shape
    hold_ref[...] = jnp.transpose(jnp.broadcast_to(gain_ref[...], (length, gain_ref.shape[1])))
    out_ref[...] = hold_ref[pl.ds(pl.multiple_of(info_ref[2] * share, 32), share), :]


def choose_body(info_ref, emb_ref, arr_ref, loss_ref, ret_ref, out_ref):
    share = emb_ref.shape[0]
    out_ref[:share] = jnp.where(info_ref[3] == 1, emb_ref[...], arr_ref[...])
    out_ref[share:] = jnp.where(info_ref[4] == 1, loss_ref[...], ret_ref[...])


def select_body(info_ref, kv_ref, four_ref, out_ref):
    out_ref[...] = jnp.where(info_ref[0] == 0, kv_ref[...], four_ref[...])


def combine_body(info_ref, own_ref, two_ref, four_ref, swap_ref, town_ref, ttwo_ref, tfour_ref):
    length = own_ref.shape[0]
    core = info_ref[0]
    late = swap_ref[:length].astype(F32)
    mid = swap_ref[length:].astype(F32)
    town_ref[...] = own_ref[...] + jnp.where(core == 0, mid, 0.0)
    ttwo_ref[...] = (two_ref[...] + late).astype(BF)
    tfour_ref[...] = (four_ref[...] + jnp.where(core == 0, 0.0, mid)).astype(BF)


def window_mask(info_ref, docs_ref, length):
    core = info_ref[0]
    index = info_ref[1]
    offsets = (0, 2, 4, 3 - 2 * core, 1 + 2 * core)
    q_row = jnp.broadcast_to(docs_ref[pl.ds(index, 1), :], (length, length))
    q_doc = jnp.transpose(q_row)
    across = lax.broadcasted_iota(jnp.int32, (length, length), 1)
    down = lax.broadcasted_iota(jnp.int32, (length, length), 0)
    masks = []
    for offset in offsets:
        block = index - offset
        k_doc = docs_ref[pl.ds(jnp.maximum(block, 0), 1), :]
        ahead = down - across + offset * length
        keep = (ahead >= 0) & (ahead < WINDOW) & (block >= 0)
        masks.append(keep & (jnp.broadcast_to(k_doc, (length, length)) == q_doc))
    return jnp.concatenate([jnp.where(m, 0.0, -1e30) for m in masks], axis=1)


def softmax_rows(q_rows, keys, bias):
    scores = dot_nt(q_rows, keys) * SCALE + bias
    top = jnp.max(scores, axis=1, keepdims=True)
    expo = jnp.exp(scores - top)
    return expo / jnp.sum(expo, axis=1, keepdims=True)


def head_rows(blocks, start):
    return jnp.concatenate([block[:, start : start + HEAD] for block in blocks], axis=0)


def attend_body(info_ref, docs_ref, q_ref, own, two, four, mid, late, wo_ref, *outs):
    length = q_ref.shape[0]
    hold_ref = outs[4]
    kv_heads = own.shape[1] // (2 * HEAD)
    groups = q_ref.shape[1] // HEAD // kv_heads
    bias = window_mask(info_ref, docs_ref, length)
    blocks = (own, two, four, mid, late)
    heads = []
    for kv in range(kv_heads):
        keys = head_rows(blocks, kv * HEAD)
        values = head_rows(blocks, (kv_heads + kv) * HEAD)
        for group in range(groups):
            head = kv * groups + group
            rows = q_ref[:, head * HEAD : (head + 1) * HEAD]
            probs = softmax_rows(rows, keys, bias).astype(BF)
            heads.append(dot_nn(probs, values).astype(BF))
    mixed = jnp.concatenate(heads, axis=1)
    whole = jnp.transpose(dot_nn(mixed, wo_ref[...]).astype(BF))
    hold_ref[...] = whole.reshape(hold_ref.shape)
    parts = hold_ref.shape[0]
    for out_ref, offset in zip(outs, SENDS):
        out_ref[...] = hold_ref[lax.rem(info_ref[2] + offset, parts)]


def attend_back_body(
    info_ref, docs_ref, q_ref, da_ref, own, two, four, mid, late,
    dq_ref, town_ref, ttwo_ref, tfour_ref, tswap_ref,
):
    length = da_ref.shape[0]
    kv_heads = own.shape[1] // (2 * HEAD)
    groups = q_ref.shape[1] // HEAD // kv_heads
    bias = window_mask(info_ref, docs_ref, length)
    blocks = (own, two, four, mid, late)
    for kv in range(kv_heads):
        at = (kv_heads + kv) * HEAD
        keys = head_rows(blocks, kv * HEAD)
        values = head_rows(blocks, at)
        d_key = d_value = 0.0
        for group in range(groups):
            head = kv * groups + group
            span = slice(head * HEAD, (head + 1) * HEAD)
            rows = q_ref[:, span]
            grad = da_ref[:, span]
            probs = softmax_rows(rows, keys, bias)
            d_value = d_value + dot_tn(probs.astype(BF), grad)
            d_probs = dot_nt(grad, values)
            delta = jnp.sum(probs * d_probs, axis=1, keepdims=True)
            d_scores = (probs * (d_probs - delta)).astype(BF)
            dq_ref[:, span] = (dot_nn(d_scores, keys) * SCALE).astype(BF)
            d_key = d_key + dot_tn(d_scores, rows)
        for terms, start in ((d_key, kv * HEAD), (d_value, at)):
            cols = slice(start, start + HEAD)
            town_ref[:, cols] = terms[:length]
            ttwo_ref[:, cols] = terms[length : 2 * length]
            tfour_ref[:, cols] = terms[2 * length : 3 * length]
            tswap_ref[:length, cols] = terms[4 * length :].astype(BF)
            tswap_ref[length:, cols] = terms[3 * length : 4 * length].astype(BF)


def input_terms_body(
    info_ref, dq_ref, own_ref, two_ref, four_ref, q_ref, kv_ref, wk_ref, wv_ref, wq_ref, *outs
):
    rows, length = outs[0].shape
    parts = len(outs)
    share = wq_ref.shape[0] // parts
    half = own_ref.shape[1] // 2
    total = own_ref[...] + two_ref[...].astype(F32) + four_ref[...].astype(F32)
    d_key = (total[:, :half] * SCALE).astype(BF)
    d_value = total[:, half:].astype(BF)
    d_query = dq_ref[...]
    row = jnp.sum(q_ref[...].astype(F32) * d_query.astype(F32), axis=1, keepdims=True)
    keys = kv_ref[:, :half].astype(F32) * d_key.astype(F32)
    values = kv_ref[:, half:].astype(F32) * d_value.astype(F32)
    row = across(row + jnp.sum(keys + values, axis=1, keepdims=True))[: rows - share]
    high = row.astype(BF).astype(F32)
    first = lax.broadcasted_iota(jnp.int32, (rows - share, length), 0) == 0
    pair = jnp.where(first, high, row - high).astype(BF)
    for out_ref, offset in zip(outs, SENDS):
        part = lax.rem(info_ref[2] + offset, parts)
        span = pl.ds(pl.multiple_of(part * share, 32), share)
        d_norm = dot_nt(wq_ref[span, :], d_query)
        d_norm = d_norm + dot_nt(wk_ref[span, :], d_key)
        d_norm = d_norm + dot_nt(wv_ref[span, :], d_value)
        out_ref[:share, :] = d_norm.astype(BF)
        out_ref[share:, :] = pair


def total_of(refs):
    return sum(ref[...].astype(F32) for ref in refs)


def finish_front_body(own, one, minus, far, both_ref, out_ref):
    share = out_ref.shape[0]
    total = total_of((own, one, minus, far))
    out_ref[...] = (both_ref[:share].astype(F32) + total).astype(BF)


def finish_body(own, one, minus, far, x_ref, both_ref, gain_ref, r_ref, out_ref):
    share = x_ref.shape[0]
    total = total_of((own, one, minus, far))
    row = (total[share : share + 1] + total[share + 1 : share + 2]) / (len(SENDS) * share)
    factor = jnp.transpose(r_ref[...])[:1]
    d_input = factor * gain_ref[...] * total[:share]
    d_input = d_input - x_ref[...].astype(F32) * (factor * factor * row)
    out_ref[...] = (both_ref[share:].astype(F32) + d_input).astype(BF)


def shifted(value, steps):
    count = lax.axis_size("seq")
    pairs = [(s, s + steps) for s in range(count) if 0 <= s + steps < count]
    return lax.ppermute(value, "seq", pairs)


def swapped(value):
    count = lax.axis_size("seq")
    return lax.ppermute(value, "seq", [(s, s ^ 1) for s in range(count)])


def next_section(value, steps):
    count = lax.axis_size("pipe")
    pairs = [(s, s + steps) for s in range(count) if 0 <= s + steps < count]
    return lax.ppermute(value, "pipe", pairs)


def exchanged(values):
    count = lax.axis_size("fsdp")
    received = []
    for value, offset in zip(values, SENDS[1:]):
        pairs = [(s, (s + offset) % count) for s in range(count)]
        received.append(lax.ppermute(value, "fsdp", pairs))
    return received


def window_blocks(info, kv):
    two = shifted(kv, 2)
    four = shifted(kv, 4)
    mine = kernel(
        select_body, 4, jax.ShapeDtypeStruct(kv.shape, BF),
        [smem()] + vmem(2), 0.5,
    )(info, kv, four)
    mid = swapped(mine)
    late = swapped(two)
    return (kv, two, four, mid, late)


def step(
    embedded, sent_forward, stashed, sent_backward, loss_grad, norm_gain,
    w_query, w_key, value_projection, w_out, forward_docs, backward_docs,
):
    length, share = embedded.shape
    parts = lax.axis_size("fsdp")
    section = lax.axis_index("pipe")
    sections = lax.axis_size("pipe")
    index = lax.axis_index("seq")
    first = (section == 0).astype(jnp.int32)
    last = (section == sections - 1).astype(jnp.int32)
    info = jnp.stack([index % 2, index, lax.axis_index("fsdp"), first, last]).astype(jnp.int32)
    gain = norm_gain
    docs_front = forward_docs[0].reshape(-1, length)
    docs_back = backward_docs[0].reshape(-1, length)
    wq, wk, wv, wo = w_query[0], w_key[0], value_projection[0], w_out[0]
    q_cols = wq.shape[1]
    kv_cols = 2 * wk.shape[1]

    def rows(count, cols, kind=BF):
        return jax.ShapeDtypeStruct((count, cols), kind)

    def pieces(count):
        return pltpu.VMEM((parts, count, length), BF)

    stash = stashed[0].T
    arrived = next_section(sent_forward[0].T, 1)
    returned = next_section(sent_backward[0].T, -1)
    gathered = exchanged((stash,) * 3)
    own_gain = kernel(
        touch_body, LIMIT, rows(share, length, F32), [smem()] + vmem(5),
        scratch=[pltpu.VMEM((parts * share, length), F32)],
    )(info, gain, wk, wv, wq, wo)

    q_back, kv_back, factor = kernel(
        project_back_body, LIMIT,
        (rows(length, q_cols), rows(length, kv_cols), rows(length, length, F32)),
        [smem()] + vmem(8), scratch=[pieces(share)],
    )(info, stash, *gathered, gain, wk, wv, wq)
    blocks_back = window_blocks(info, kv_back)

    sent = kernel(
        choose_body, LIMIT, rows(2 * share, length), [smem()] + vmem(4), 1.0,
    )(info, embedded.T, arrived, loss_grad.T, returned)
    both = exchanged((sent,) * 3)
    q_front, kv_front, d_attn = kernel(
        project_front_body, LIMIT,
        (rows(length, q_cols), rows(length, kv_cols), rows(length, q_cols)),
        [smem()] + vmem(9), scratch=[pieces(2 * share)],
    )(info, sent, *both, gain, wk, wv, wq, wo)
    blocks_front = window_blocks(info, kv_front)

    terms = rows(length, kv_cols, F32)
    d_query, t_own, t_two, t_four, t_swap = kernel(
        attend_back_body, LIMIT,
        (rows(length, q_cols), terms, terms, terms, rows(2 * length, kv_cols)),
        [smem()] + vmem(8),
    )(info, docs_back, q_back, d_attn, *blocks_back)
    t_swap = swapped(t_swap)
    t_own, send_two, send_four = kernel(
        combine_body, LIMIT, (terms, rows(length, kv_cols), rows(length, kv_cols)),
        [smem()] + vmem(4), 1.0,
    )(info, t_own, t_two, t_four, t_swap)
    back_two = shifted(send_two, -2)
    back_four = shifted(send_four, -4)

    partial_out = kernel(
        attend_body, LIMIT, (rows(share, length),) * 4, [smem()] + vmem(8),
        scratch=[pieces(share)],
    )(info, docs_front, q_front, *blocks_front, wo)
    sums = exchanged(partial_out[1:])
    forward_out = kernel(finish_front_body, 8, rows(share, length), vmem(5), 1.0)(
        partial_out[0], *sums, sent
    )

    d_parts = kernel(
        input_terms_body, LIMIT, (rows(share + 16, length),) * 4,
        [smem()] + vmem(9),
    )(info, d_query, t_own, back_two, back_four, q_back, kv_back, wk, wv, wq)
    sums = exchanged(d_parts[1:])
    input_grad = kernel(finish_body, 8, rows(share, length), vmem(8), 1.0)(
        d_parts[0], *sums, stash, sent, own_gain, factor
    )
    return (forward_out.T[None], input_grad.T[None])


def solution(mesh):
    placed = (
        P("seq", "fsdp"),
        P("pipe", "seq", "fsdp"),
        P("pipe", "seq", "fsdp"),
        P("pipe", "seq", "fsdp"),
        P("seq", "fsdp"),
        P("pipe", None),
        P("pipe", None, "fsdp"),
        P("pipe", None, "fsdp"),
        P("pipe", None, "fsdp"),
        P("pipe", "fsdp", None),
        P("pipe", None),
        P("pipe", None),
    )
    return jax.shard_map(
        step,
        mesh=mesh,
        in_specs=placed,
        out_specs=(P("pipe", "seq", "fsdp"), P("pipe", "seq", "fsdp")),
        check_vma=False,
    )
```

```python
import jax
import jax.numpy as jnp
from jax import lax
from jax.experimental import pallas as pl
from jax.experimental.pallas import tpu as pltpu
from jax.sharding import PartitionSpec as P


HEAD = 128
WINDOW = 512
SCALE = HEAD ** (-0.5)
BF = jnp.bfloat16
F32 = jnp.float32
LIMIT = 14
SENDS = (0, 1, 3, 2)


def dot_nn(left, right):
    return lax.dot_general(left, right, (((1,), (0,)), ((), ())), preferred_element_type=F32)


def dot_nt(left, right):
    return lax.dot_general(left, right, (((1,), (1,)), ((), ())), preferred_element_type=F32)


def dot_tn(left, right):
    return lax.dot_general(left, right, (((0,), (0,)), ((), ())), preferred_element_type=F32)


def vmem(count):
    return [pl.BlockSpec(memory_space=pltpu.VMEM) for _ in range(count)]


def smem():
    return pl.BlockSpec(memory_space=pltpu.SMEM)


def limit(mebibytes):
    return pltpu.CompilerParams(vmem_limit_bytes=mebibytes * 2**20)


def cost(microseconds):
    return pl.CostEstimate(
        flops=0, transcendentals=0, bytes_accessed=int(microseconds * 3_300_000)
    )


def kernel(body, mebibytes, out_shape, in_specs, microseconds=4.0, scratch=()):
    single = not isinstance(out_shape, tuple)
    return pl.pallas_call(
        body,
        out_shape=out_shape,
        in_specs=in_specs,
        out_specs=vmem(1)[0] if single else tuple(vmem(len(out_shape))),
        scratch_shapes=scratch,
        compiler_params=limit(mebibytes),
        cost_estimate=cost(microseconds),
    )


def stacked(ref, start, share):
    return jnp.concatenate([ref[part, start : start + share, :] for part in range(ref.shape[0])], 0)


def normal_rows(value, gain_ref):
    value = jnp.transpose(value).astype(F32)
    mean = jnp.mean(value * value, axis=1, keepdims=True)
    factor = lax.rsqrt(mean + 1e-06)
    return (value * factor * gain_ref[...]).astype(BF), factor


def across(column):
    length = column.shape[0]
    return jnp.transpose(jnp.broadcast_to(column, (length, length)))


def project_rows(h, wk_ref, wv_ref, wq_ref, q_ref, kv_ref):
    half = kv_ref.shape[1] // 2
    kv_ref[:, :half] = dot_nn(h, wk_ref[...]).astype(BF)
    kv_ref[:, half:] = dot_nn(h, wv_ref[...]).astype(BF)
    q_ref[...] = dot_nn(h, wq_ref[...]).astype(BF)


def placed_parts(info_ref, own, one, minus, far, hold_ref):
    place = info_ref[2]
    parts = hold_ref.shape[0]
    for offset, piece in ((0, own), (parts - 1, one), (1, minus), (2, far)):
        hold_ref[lax.rem(place + offset, parts)] = piece[...]


def spread_body(x_ref, out_ref):
    for part in range(out_ref.shape[0]):
        out_ref[part] = x_ref[...]


def project_back_body(x_ref, gain_ref, wk_ref, wv_ref, wq_ref, q_ref, kv_ref, r_ref):
    h, factor = normal_rows(stacked(x_ref, 0, x_ref.shape[1]), gain_ref)
    r_ref[...] = jnp.broadcast_to(factor, r_ref.shape)
    project_rows(h, wk_ref, wv_ref, wq_ref, q_ref, kv_ref)


def project_front_body(
    info_ref, own, one, minus, far, gain_ref, wk_ref, wv_ref, wq_ref, wo_ref,
    q_ref, kv_ref, da_ref, hold_ref,
):
    placed_parts(info_ref, own, one, minus, far, hold_ref)
    share = hold_ref.shape[1] // 2
    h, _ = normal_rows(stacked(hold_ref, 0, share), gain_ref)
    project_rows(h, wk_ref, wv_ref, wq_ref, q_ref, kv_ref)
    grad = dot_nn(wo_ref[...], stacked(hold_ref, share, share))
    da_ref[...] = jnp.transpose(grad.astype(BF))


def touch_body(info_ref, gain_ref, out_ref, hold_ref):
    share, length = out_ref.shape
    hold_ref[...] = jnp.transpose(jnp.broadcast_to(gain_ref[...], (length, gain_ref.shape[1])))
    out_ref[...] = hold_ref[pl.ds(pl.multiple_of(info_ref[2] * share, 32), share), :]


def choose_body(info_ref, emb_ref, arr_ref, loss_ref, ret_ref, out_ref):
    share = emb_ref.shape[0]
    out_ref[:share] = jnp.where(info_ref[3] == 1, emb_ref[...], arr_ref[...])
    out_ref[share:] = jnp.where(info_ref[4] == 1, loss_ref[...], ret_ref[...])


def select_body(info_ref, kv_ref, four_ref, out_ref):
    out_ref[...] = jnp.where(info_ref[0] == 0, kv_ref[...], four_ref[...])


def combine_body(info_ref, own_ref, two_ref, four_ref, swap_ref, town_ref, ttwo_ref, tfour_ref):
    length = own_ref.shape[0]
    core = info_ref[0]
    late = swap_ref[:length].astype(F32)
    mid = swap_ref[length:].astype(F32)
    town_ref[...] = own_ref[...] + jnp.where(core == 0, mid, 0.0)
    ttwo_ref[...] = (two_ref[...] + late).astype(BF)
    tfour_ref[...] = (four_ref[...] + jnp.where(core == 0, 0.0, mid)).astype(BF)


def window_mask(info_ref, docs_ref, length):
    core = info_ref[0]
    index = info_ref[1]
    offsets = (0, 2, 4, 3 - 2 * core, 1 + 2 * core)
    q_row = jnp.broadcast_to(docs_ref[pl.ds(index, 1), :], (length, length))
    q_doc = jnp.transpose(q_row)
    across = lax.broadcasted_iota(jnp.int32, (length, length), 1)
    down = lax.broadcasted_iota(jnp.int32, (length, length), 0)
    masks = []
    for offset in offsets:
        block = index - offset
        k_doc = docs_ref[pl.ds(jnp.maximum(block, 0), 1), :]
        ahead = down - across + offset * length
        keep = (ahead >= 0) & (ahead < WINDOW) & (block >= 0)
        masks.append(keep & (jnp.broadcast_to(k_doc, (length, length)) == q_doc))
    return jnp.concatenate([jnp.where(m, 0.0, -1e30) for m in masks], axis=1)


def softmax_rows(q_rows, keys, bias):
    scores = dot_nt(q_rows, keys) * SCALE + bias
    top = jnp.max(scores, axis=1, keepdims=True)
    expo = jnp.exp(scores - top)
    return expo / jnp.sum(expo, axis=1, keepdims=True)


def head_rows(blocks, start):
    return jnp.concatenate([block[:, start : start + HEAD] for block in blocks], axis=0)


def attend_body(info_ref, docs_ref, q_ref, own, two, four, mid, late, wo_ref, *outs):
    length = q_ref.shape[0]
    hold_ref = outs[4]
    kv_heads = own.shape[1] // (2 * HEAD)
    groups = q_ref.shape[1] // HEAD // kv_heads
    bias = window_mask(info_ref, docs_ref, length)
    blocks = (own, two, four, mid, late)
    heads = []
    for kv in range(kv_heads):
        keys = head_rows(blocks, kv * HEAD)
        values = head_rows(blocks, (kv_heads + kv) * HEAD)
        for group in range(groups):
            head = kv * groups + group
            rows = q_ref[:, head * HEAD : (head + 1) * HEAD]
            probs = softmax_rows(rows, keys, bias).astype(BF)
            heads.append(dot_nn(probs, values).astype(BF))
    mixed = jnp.concatenate(heads, axis=1)
    whole = jnp.transpose(dot_nn(mixed, wo_ref[...]).astype(BF))
    hold_ref[...] = whole.reshape(hold_ref.shape)
    parts = hold_ref.shape[0]
    for out_ref, offset in zip(outs, SENDS):
        out_ref[...] = hold_ref[lax.rem(info_ref[2] + offset, parts)]


def attend_back_body(
    info_ref, docs_ref, q_ref, da_ref, own, two, four, mid, late,
    dq_ref, town_ref, ttwo_ref, tfour_ref, tswap_ref,
):
    length = da_ref.shape[0]
    kv_heads = own.shape[1] // (2 * HEAD)
    groups = q_ref.shape[1] // HEAD // kv_heads
    bias = window_mask(info_ref, docs_ref, length)
    blocks = (own, two, four, mid, late)
    for kv in range(kv_heads):
        at = (kv_heads + kv) * HEAD
        keys = head_rows(blocks, kv * HEAD)
        values = head_rows(blocks, at)
        d_key = d_value = 0.0
        for group in range(groups):
            head = kv * groups + group
            span = slice(head * HEAD, (head + 1) * HEAD)
            rows = q_ref[:, span]
            grad = da_ref[:, span]
            probs = softmax_rows(rows, keys, bias)
            d_value = d_value + dot_tn(probs.astype(BF), grad)
            d_probs = dot_nt(grad, values)
            delta = jnp.sum(probs * d_probs, axis=1, keepdims=True)
            d_scores = (probs * (d_probs - delta)).astype(BF)
            dq_ref[:, span] = (dot_nn(d_scores, keys) * SCALE).astype(BF)
            d_key = d_key + dot_tn(d_scores, rows)
        for terms, start in ((d_key, kv * HEAD), (d_value, at)):
            cols = slice(start, start + HEAD)
            town_ref[:, cols] = terms[:length]
            ttwo_ref[:, cols] = terms[length : 2 * length]
            tfour_ref[:, cols] = terms[2 * length : 3 * length]
            tswap_ref[:length, cols] = terms[4 * length :].astype(BF)
            tswap_ref[length:, cols] = terms[3 * length : 4 * length].astype(BF)


def input_terms_body(
    info_ref, dq_ref, own_ref, two_ref, four_ref, q_ref, kv_ref, wk_ref, wv_ref, wq_ref, *outs
):
    rows, length = outs[0].shape
    parts = len(outs)
    share = wq_ref.shape[0] // parts
    half = own_ref.shape[1] // 2
    total = own_ref[...] + two_ref[...].astype(F32) + four_ref[...].astype(F32)
    d_key = (total[:, :half] * SCALE).astype(BF)
    d_value = total[:, half:].astype(BF)
    d_query = dq_ref[...]
    row = jnp.sum(q_ref[...].astype(F32) * d_query.astype(F32), axis=1, keepdims=True)
    keys = kv_ref[:, :half].astype(F32) * d_key.astype(F32)
    values = kv_ref[:, half:].astype(F32) * d_value.astype(F32)
    row = across(row + jnp.sum(keys + values, axis=1, keepdims=True))[: rows - share]
    high = row.astype(BF).astype(F32)
    first = lax.broadcasted_iota(jnp.int32, (rows - share, length), 0) == 0
    pair = jnp.where(first, high, row - high).astype(BF)
    for out_ref, offset in zip(outs, SENDS):
        part = lax.rem(info_ref[2] + offset, parts)
        span = pl.ds(pl.multiple_of(part * share, 32), share)
        d_norm = dot_nt(wq_ref[span, :], d_query)
        d_norm = d_norm + dot_nt(wk_ref[span, :], d_key)
        d_norm = d_norm + dot_nt(wv_ref[span, :], d_value)
        out_ref[:share, :] = d_norm.astype(BF)
        out_ref[share:, :] = pair


def total_of(refs):
    return sum(ref[...].astype(F32) for ref in refs)


def finish_front_body(own, one, minus, far, both_ref, out_ref):
    share = out_ref.shape[0]
    total = total_of((own, one, minus, far))
    out_ref[...] = (both_ref[:share].astype(F32) + total).astype(BF)


def finish_body(own, one, minus, far, x_ref, both_ref, gain_ref, r_ref, out_ref):
    share = x_ref.shape[0]
    total = total_of((own, one, minus, far))
    row = (total[share : share + 1] + total[share + 1 : share + 2]) / (len(SENDS) * share)
    factor = jnp.transpose(r_ref[...])[:1]
    d_input = factor * gain_ref[...] * total[:share]
    d_input = d_input - x_ref[...].astype(F32) * (factor * factor * row)
    out_ref[...] = (both_ref[share:].astype(F32) + d_input).astype(BF)


def shifted(value, steps):
    count = lax.axis_size("seq")
    pairs = [(s, s + steps) for s in range(count) if 0 <= s + steps < count]
    return lax.ppermute(value, "seq", pairs)


def swapped(value):
    count = lax.axis_size("seq")
    return lax.ppermute(value, "seq", [(s, s ^ 1) for s in range(count)])


def next_section(value, steps):
    count = lax.axis_size("pipe")
    pairs = [(s, s + steps) for s in range(count) if 0 <= s + steps < count]
    return lax.ppermute(value, "pipe", pairs)


def exchanged(values):
    count = lax.axis_size("fsdp")
    received = []
    for value, offset in zip(values, SENDS[1:]):
        pairs = [(s, (s + offset) % count) for s in range(count)]
        received.append(lax.ppermute(value, "fsdp", pairs))
    return received


def window_blocks(info, kv):
    two = shifted(kv, 2)
    four = shifted(kv, 4)
    mine = kernel(
        select_body, 4, jax.ShapeDtypeStruct(kv.shape, BF),
        [smem()] + vmem(2), 0.5,
    )(info, kv, four)
    mid = swapped(mine)
    late = swapped(two)
    return (kv, two, four, mid, late)


def step(
    embedded, sent_forward, stashed, sent_backward, loss_grad, norm_gain,
    w_query, w_key, value_projection, w_out, forward_docs, backward_docs,
):
    length, share = embedded.shape
    parts = lax.axis_size("fsdp")
    section = lax.axis_index("pipe")
    sections = lax.axis_size("pipe")
    index = lax.axis_index("seq")
    first = (section == 0).astype(jnp.int32)
    last = (section == sections - 1).astype(jnp.int32)
    info = jnp.stack([index % 2, index, lax.axis_index("fsdp"), first, last]).astype(jnp.int32)
    gain = norm_gain
    docs_front = forward_docs[0].reshape(-1, length)
    docs_back = backward_docs[0].reshape(-1, length)
    wq, wk, wv, wo = w_query[0], w_key[0], value_projection[0], w_out[0]
    q_cols = wq.shape[1]
    kv_cols = 2 * wk.shape[1]

    def rows(count, cols, kind=BF):
        return jax.ShapeDtypeStruct((count, cols), kind)

    def pieces(count):
        return pltpu.VMEM((parts, count, length), BF)

    stash, ahead, behind, info = lax.optimization_barrier(
        (stashed[0].T, sent_forward[0].T, sent_backward[0].T, info)
    )
    arrived = next_section(ahead, 1)
    returned = next_section(behind, -1)
    spread = kernel(
        spread_body, 4, jax.ShapeDtypeStruct((parts, share, length), BF), vmem(1), 1.0
    )(stash)
    gathered = lax.all_to_all(spread, "fsdp", 0, 0)
    own_gain = kernel(
        touch_body, LIMIT, rows(share, length, F32), [smem()] + vmem(1),
        scratch=[pltpu.VMEM((parts * share, length), F32)],
    )(info, gain)

    q_back, kv_back, factor = kernel(
        project_back_body, LIMIT,
        (rows(length, q_cols), rows(length, kv_cols), rows(length, length, F32)),
        vmem(5),
    )(gathered, gain, wk, wv, wq)
    blocks_back = window_blocks(info, kv_back)

    sent = kernel(
        choose_body, LIMIT, rows(2 * share, length), [smem()] + vmem(4), 20.0,
    )(info, embedded.T, arrived, loss_grad.T, returned)
    both = exchanged((sent,) * 3)
    q_front, kv_front, d_attn = kernel(
        project_front_body, LIMIT,
        (rows(length, q_cols), rows(length, kv_cols), rows(length, q_cols)),
        [smem()] + vmem(9), scratch=[pieces(2 * share)],
    )(info, sent, *both, gain, wk, wv, wq, wo)
    blocks_front = window_blocks(info, kv_front)

    terms = rows(length, kv_cols, F32)
    d_query, t_own, t_two, t_four, t_swap = kernel(
        attend_back_body, LIMIT,
        (rows(length, q_cols), terms, terms, terms, rows(2 * length, kv_cols)),
        [smem()] + vmem(8),
    )(info, docs_back, q_back, d_attn, *blocks_back)
    t_swap = swapped(t_swap)
    t_own, send_two, send_four = kernel(
        combine_body, LIMIT, (terms, rows(length, kv_cols), rows(length, kv_cols)),
        [smem()] + vmem(4), 1.0,
    )(info, t_own, t_two, t_four, t_swap)
    back_two = shifted(send_two, -2)
    back_four = shifted(send_four, -4)

    partial_out = kernel(
        attend_body, LIMIT, (rows(share, length),) * 4, [smem()] + vmem(8),
        scratch=[pieces(share)],
    )(info, docs_front, q_front, *blocks_front, wo)
    sums = exchanged(partial_out[1:])
    forward_out = kernel(finish_front_body, 8, rows(share, length), vmem(5), 1.0)(
        partial_out[0], *sums, sent
    )

    d_parts = kernel(
        input_terms_body, LIMIT, (rows(share + 16, length),) * 4,
        [smem()] + vmem(9),
    )(info, d_query, t_own, back_two, back_four, q_back, kv_back, wk, wv, wq)
    sums = exchanged(d_parts[1:])
    input_grad = kernel(finish_body, 8, rows(share, length), vmem(8), 1.0)(
        d_parts[0], *sums, stash, sent, own_gain, factor
    )
    return (forward_out.T[None], input_grad.T[None])


def solution(mesh):
    placed = (
        P("seq", "fsdp"),
        P("pipe", "seq", "fsdp"),
        P("pipe", "seq", "fsdp"),
        P("pipe", "seq", "fsdp"),
        P("seq", "fsdp"),
        P("pipe", None),
        P("pipe", None, "fsdp"),
        P("pipe", None, "fsdp"),
        P("pipe", None, "fsdp"),
        P("pipe", "fsdp", None),
        P("pipe", None),
        P("pipe", None),
    )
    return jax.shard_map(
        step,
        mesh=mesh,
        in_specs=placed,
        out_specs=(P("pipe", "seq", "fsdp"), P("pipe", "seq", "fsdp")),
        check_vma=False,
    )
```

```python
import jax
import jax.numpy as jnp
from jax import lax
from jax.experimental import pallas as pl
from jax.experimental.pallas import tpu as pltpu
from jax.sharding import PartitionSpec as P


HEAD = 128
WINDOW = 512
SCALE = HEAD ** (-0.5)
BF = jnp.bfloat16
F32 = jnp.float32
LIMIT = 14
SENDS = (0, 1, 3, 2)


def dot_nn(left, right):
    return lax.dot_general(left, right, (((1,), (0,)), ((), ())), preferred_element_type=F32)


def dot_nt(left, right):
    return lax.dot_general(left, right, (((1,), (1,)), ((), ())), preferred_element_type=F32)


def dot_tn(left, right):
    return lax.dot_general(left, right, (((0,), (0,)), ((), ())), preferred_element_type=F32)


def vmem(count):
    return [pl.BlockSpec(memory_space=pltpu.VMEM) for _ in range(count)]


def any_space():
    return pl.BlockSpec(memory_space=pl.ANY)


def smem():
    return pl.BlockSpec(memory_space=pltpu.SMEM)


def limit(mebibytes):
    return pltpu.CompilerParams(vmem_limit_bytes=mebibytes * 2**20)


def cost(microseconds):
    return pl.CostEstimate(
        flops=0, transcendentals=0, bytes_accessed=int(microseconds * 3_300_000)
    )


def kernel(body, mebibytes, out_shape, in_specs, microseconds=4.0, scratch=()):
    single = not isinstance(out_shape, tuple)
    return pl.pallas_call(
        body,
        out_shape=out_shape,
        in_specs=in_specs,
        out_specs=vmem(1)[0] if single else tuple(vmem(len(out_shape))),
        scratch_shapes=scratch,
        compiler_params=limit(mebibytes),
        cost_estimate=cost(microseconds),
    )


def stacked(ref, start, share):
    return jnp.concatenate([ref[part, start : start + share, :] for part in range(ref.shape[0])], 0)


def normal_rows(value, gain_ref):
    value = jnp.transpose(value).astype(F32)
    mean = jnp.mean(value * value, axis=1, keepdims=True)
    factor = lax.rsqrt(mean + 1e-06)
    return (value * factor * gain_ref[...]).astype(BF), factor


def across(column):
    length = column.shape[0]
    return jnp.transpose(jnp.broadcast_to(column, (length, length)))


def project_rows(h, wk_ref, wv_ref, wq_ref, q_ref, kv_ref):
    half = kv_ref.shape[1] // 2
    kv_ref[:, :half] = dot_nn(h, wk_ref[...]).astype(BF)
    kv_ref[:, half:] = dot_nn(h, wv_ref[...]).astype(BF)
    q_ref[...] = dot_nn(h, wq_ref[...]).astype(BF)


def placed_parts(info_ref, own, one, minus, far, hold_ref):
    place = info_ref[2]
    parts = hold_ref.shape[0]
    for offset, piece in ((0, own), (parts - 1, one), (1, minus), (2, far)):
        hold_ref[lax.rem(place + offset, parts)] = piece[...]


def spread_body(x_ref, out_ref, sems):
    copies = [
        pltpu.make_async_copy(x_ref, out_ref.at[part], sems.at[part])
        for part in range(out_ref.shape[0])
    ]
    for copy in copies:
        copy.start()
    for copy in copies:
        copy.wait()


def project_back_body(x_ref, gain_ref, wk_ref, wv_ref, wq_ref, q_ref, kv_ref, r_ref):
    h, factor = normal_rows(stacked(x_ref, 0, x_ref.shape[1]), gain_ref)
    r_ref[...] = jnp.broadcast_to(factor, r_ref.shape)
    project_rows(h, wk_ref, wv_ref, wq_ref, q_ref, kv_ref)


def project_front_body(
    info_ref, own, one, minus, far, gain_ref, wk_ref, wv_ref, wq_ref, wo_ref,
    q_ref, kv_ref, da_ref, hold_ref,
):
    placed_parts(info_ref, own, one, minus, far, hold_ref)
    share = hold_ref.shape[1] // 2
    h, _ = normal_rows(stacked(hold_ref, 0, share), gain_ref)
    project_rows(h, wk_ref, wv_ref, wq_ref, q_ref, kv_ref)
    grad = dot_nn(wo_ref[...], stacked(hold_ref, share, share))
    da_ref[...] = jnp.transpose(grad.astype(BF))


def touch_body(info_ref, gain_ref, out_ref, hold_ref):
    share, length = out_ref.shape
    hold_ref[...] = jnp.transpose(jnp.broadcast_to(gain_ref[...], (length, gain_ref.shape[1])))
    out_ref[...] = hold_ref[pl.ds(pl.multiple_of(info_ref[2] * share, 32), share), :]


def choose_body(info_ref, emb_ref, arr_ref, loss_ref, ret_ref, out_ref):
    share = emb_ref.shape[0]
    out_ref[:share] = jnp.where(info_ref[3] == 1, emb_ref[...], arr_ref[...])
    out_ref[share:] = jnp.where(info_ref[4] == 1, loss_ref[...], ret_ref[...])


def select_body(info_ref, kv_ref, four_ref, out_ref):
    out_ref[...] = jnp.where(info_ref[0] == 0, kv_ref[...], four_ref[...])


def combine_body(info_ref, own_ref, two_ref, four_ref, swap_ref, town_ref, ttwo_ref, tfour_ref):
    length = own_ref.shape[0]
    core = info_ref[0]
    late = swap_ref[:length].astype(F32)
    mid = swap_ref[length:].astype(F32)
    town_ref[...] = own_ref[...] + jnp.where(core == 0, mid, 0.0)
    ttwo_ref[...] = (two_ref[...] + late).astype(BF)
    tfour_ref[...] = (four_ref[...] + jnp.where(core == 0, 0.0, mid)).astype(BF)


def window_mask(info_ref, docs_ref, length):
    core = info_ref[0]
    index = info_ref[1]
    offsets = (0, 2, 4, 3 - 2 * core, 1 + 2 * core)
    q_row = jnp.broadcast_to(docs_ref[pl.ds(index, 1), :], (length, length))
    q_doc = jnp.transpose(q_row)
    across = lax.broadcasted_iota(jnp.int32, (length, length), 1)
    down = lax.broadcasted_iota(jnp.int32, (length, length), 0)
    masks = []
    for offset in offsets:
        block = index - offset
        k_doc = docs_ref[pl.ds(jnp.maximum(block, 0), 1), :]
        ahead = down - across + offset * length
        keep = (ahead >= 0) & (ahead < WINDOW) & (block >= 0)
        masks.append(keep & (jnp.broadcast_to(k_doc, (length, length)) == q_doc))
    return jnp.concatenate([jnp.where(m, 0.0, -1e30) for m in masks], axis=1)


def softmax_rows(q_rows, keys, bias):
    scores = dot_nt(q_rows, keys) * SCALE + bias
    top = jnp.max(scores, axis=1, keepdims=True)
    expo = jnp.exp(scores - top)
    return expo / jnp.sum(expo, axis=1, keepdims=True)


def head_rows(blocks, start):
    return jnp.concatenate([block[:, start : start + HEAD] for block in blocks], axis=0)


def attend_body(info_ref, docs_ref, q_ref, own, two, four, mid, late, wo_ref, *outs):
    length = q_ref.shape[0]
    hold_ref = outs[4]
    kv_heads = own.shape[1] // (2 * HEAD)
    groups = q_ref.shape[1] // HEAD // kv_heads
    bias = window_mask(info_ref, docs_ref, length)
    blocks = (own, two, four, mid, late)
    heads = []
    for kv in range(kv_heads):
        keys = head_rows(blocks, kv * HEAD)
        values = head_rows(blocks, (kv_heads + kv) * HEAD)
        for group in range(groups):
            head = kv * groups + group
            rows = q_ref[:, head * HEAD : (head + 1) * HEAD]
            probs = softmax_rows(rows, keys, bias).astype(BF)
            heads.append(dot_nn(probs, values).astype(BF))
    mixed = jnp.concatenate(heads, axis=1)
    whole = jnp.transpose(dot_nn(mixed, wo_ref[...]).astype(BF))
    hold_ref[...] = whole.reshape(hold_ref.shape)
    parts = hold_ref.shape[0]
    for out_ref, offset in zip(outs, SENDS):
        out_ref[...] = hold_ref[lax.rem(info_ref[2] + offset, parts)]


def attend_back_body(
    info_ref, docs_ref, q_ref, da_ref, own, two, four, mid, late,
    dq_ref, town_ref, ttwo_ref, tfour_ref, tswap_ref,
):
    length = da_ref.shape[0]
    kv_heads = own.shape[1] // (2 * HEAD)
    groups = q_ref.shape[1] // HEAD // kv_heads
    bias = window_mask(info_ref, docs_ref, length)
    blocks = (own, two, four, mid, late)
    for kv in range(kv_heads):
        at = (kv_heads + kv) * HEAD
        keys = head_rows(blocks, kv * HEAD)
        values = head_rows(blocks, at)
        d_key = d_value = 0.0
        for group in range(groups):
            head = kv * groups + group
            span = slice(head * HEAD, (head + 1) * HEAD)
            rows = q_ref[:, span]
            grad = da_ref[:, span]
            probs = softmax_rows(rows, keys, bias)
            d_value = d_value + dot_tn(probs.astype(BF), grad)
            d_probs = dot_nt(grad, values)
            delta = jnp.sum(probs * d_probs, axis=1, keepdims=True)
            d_scores = (probs * (d_probs - delta)).astype(BF)
            dq_ref[:, span] = (dot_nn(d_scores, keys) * SCALE).astype(BF)
            d_key = d_key + dot_tn(d_scores, rows)
        for terms, start in ((d_key, kv * HEAD), (d_value, at)):
            cols = slice(start, start + HEAD)
            town_ref[:, cols] = terms[:length]
            ttwo_ref[:, cols] = terms[length : 2 * length]
            tfour_ref[:, cols] = terms[2 * length : 3 * length]
            tswap_ref[:length, cols] = terms[4 * length :].astype(BF)
            tswap_ref[length:, cols] = terms[3 * length : 4 * length].astype(BF)


def input_terms_body(
    dq_ref, own_ref, two_ref, four_ref, q_ref, kv_ref, wk_ref, wv_ref, wq_ref, out_ref
):
    parts, rows, length = out_ref.shape
    share = wq_ref.shape[0] // parts
    half = own_ref.shape[1] // 2
    total = own_ref[...] + two_ref[...].astype(F32) + four_ref[...].astype(F32)
    d_key = (total[:, :half] * SCALE).astype(BF)
    d_value = total[:, half:].astype(BF)
    d_query = dq_ref[...]
    row = jnp.sum(q_ref[...].astype(F32) * d_query.astype(F32), axis=1, keepdims=True)
    keys = kv_ref[:, :half].astype(F32) * d_key.astype(F32)
    values = kv_ref[:, half:].astype(F32) * d_value.astype(F32)
    row = across(row + jnp.sum(keys + values, axis=1, keepdims=True))[: rows - share]
    high = row.astype(BF).astype(F32)
    first = lax.broadcasted_iota(jnp.int32, (rows - share, length), 0) == 0
    pair = jnp.where(first, high, row - high).astype(BF)
    for part in range(parts):
        span = slice(part * share, (part + 1) * share)
        d_norm = dot_nt(wq_ref[span], d_query)
        d_norm = d_norm + dot_nt(wk_ref[span], d_key)
        d_norm = d_norm + dot_nt(wv_ref[span], d_value)
        out_ref[part, :share] = d_norm.astype(BF)
        out_ref[part, share:] = pair


def total_of(refs):
    return sum(ref[...].astype(F32) for ref in refs)


def finish_front_body(own, one, minus, far, both_ref, out_ref):
    share = out_ref.shape[0]
    total = total_of((own, one, minus, far))
    out_ref[...] = (both_ref[:share].astype(F32) + total).astype(BF)


def finish_body(sums_ref, x_ref, both_ref, gain_ref, r_ref, out_ref):
    share = x_ref.shape[0]
    parts = sums_ref.shape[0]
    total = sum(sums_ref[part].astype(F32) for part in range(parts))
    row = (total[share : share + 1] + total[share + 1 : share + 2]) / (parts * share)
    factor = jnp.transpose(r_ref[...])[:1]
    d_input = factor * gain_ref[...] * total[:share]
    d_input = d_input - x_ref[...].astype(F32) * (factor * factor * row)
    out_ref[...] = (both_ref[share:].astype(F32) + d_input).astype(BF)


def shifted(value, steps):
    count = lax.axis_size("seq")
    pairs = [(s, s + steps) for s in range(count) if 0 <= s + steps < count]
    return lax.ppermute(value, "seq", pairs)


def swapped(value):
    count = lax.axis_size("seq")
    return lax.ppermute(value, "seq", [(s, s ^ 1) for s in range(count)])


def next_section(value, steps):
    count = lax.axis_size("pipe")
    pairs = [(s, s + steps) for s in range(count) if 0 <= s + steps < count]
    return lax.ppermute(value, "pipe", pairs)


def exchanged(values):
    count = lax.axis_size("fsdp")
    received = []
    for value, offset in zip(values, SENDS[1:]):
        pairs = [(s, (s + offset) % count) for s in range(count)]
        received.append(lax.ppermute(value, "fsdp", pairs))
    return received


def window_blocks(info, kv):
    two = shifted(kv, 2)
    four = shifted(kv, 4)
    mine = kernel(
        select_body, 4, jax.ShapeDtypeStruct(kv.shape, BF),
        [smem()] + vmem(2), 0.5,
    )(info, kv, four)
    mid = swapped(mine)
    late = swapped(two)
    return (kv, two, four, mid, late)


def step(
    embedded, sent_forward, stashed, sent_backward, loss_grad, norm_gain,
    w_query, w_key, value_projection, w_out, forward_docs, backward_docs,
):
    length, share = embedded.shape
    parts = lax.axis_size("fsdp")
    section = lax.axis_index("pipe")
    sections = lax.axis_size("pipe")
    index = lax.axis_index("seq")
    first = (section == 0).astype(jnp.int32)
    last = (section == sections - 1).astype(jnp.int32)
    info = jnp.stack([index % 2, index, lax.axis_index("fsdp"), first, last]).astype(jnp.int32)
    gain = norm_gain
    docs_front = forward_docs[0].reshape(-1, length)
    docs_back = backward_docs[0].reshape(-1, length)
    wq, wk, wv, wo = w_query[0], w_key[0], value_projection[0], w_out[0]
    q_cols = wq.shape[1]
    kv_cols = 2 * wk.shape[1]

    def rows(count, cols, kind=BF):
        return jax.ShapeDtypeStruct((count, cols), kind)

    def pieces(count):
        return pltpu.VMEM((parts, count, length), BF)

    stash, ahead, behind, info = lax.optimization_barrier(
        (stashed[0].T, sent_forward[0].T, sent_backward[0].T, info)
    )
    arrived = next_section(ahead, 1)
    returned = next_section(behind, -1)
    spread = pl.pallas_call(
        spread_body,
        out_shape=jax.ShapeDtypeStruct((parts, share, length), BF),
        in_specs=[any_space()], out_specs=any_space(),
        scratch_shapes=[pltpu.SemaphoreType.DMA((parts,))],
        name="spread", compiler_params=limit(4), cost_estimate=cost(1.0),
    )(stash)
    gathered = lax.all_to_all(spread, "fsdp", 0, 0)
    own_gain = kernel(
        touch_body, LIMIT, rows(share, length, F32), [smem()] + vmem(1),
        scratch=[pltpu.VMEM((parts * share, length), F32)],
    )(info, gain)

    q_back, kv_back, factor = kernel(
        project_back_body, LIMIT,
        (rows(length, q_cols), rows(length, kv_cols), rows(length, length, F32)),
        vmem(5),
    )(gathered, gain, wk, wv, wq)
    blocks_back = window_blocks(info, kv_back)

    sent = kernel(
        choose_body, LIMIT, rows(2 * share, length), [smem()] + vmem(4), 4.0,
    )(info, embedded.T, arrived, loss_grad.T, returned)
    both = exchanged((sent,) * 3)
    q_front, kv_front, d_attn = kernel(
        project_front_body, LIMIT,
        (rows(length, q_cols), rows(length, kv_cols), rows(length, q_cols)),
        [smem()] + vmem(9), scratch=[pieces(2 * share)],
    )(info, sent, *both, gain, wk, wv, wq, wo)
    blocks_front = window_blocks(info, kv_front)

    terms = rows(length, kv_cols, F32)
    d_query, t_own, t_two, t_four, t_swap = kernel(
        attend_back_body, LIMIT,
        (rows(length, q_cols), terms, terms, terms, rows(2 * length, kv_cols)),
        [smem()] + vmem(8),
    )(info, docs_back, q_back, d_attn, *blocks_back)
    t_swap = swapped(t_swap)
    t_own, send_two, send_four = kernel(
        combine_body, LIMIT, (terms, rows(length, kv_cols), rows(length, kv_cols)),
        [smem()] + vmem(4), 1.0,
    )(info, t_own, t_two, t_four, t_swap)
    back_two = shifted(send_two, -2)
    back_four = shifted(send_four, -4)

    partial_out = kernel(
        attend_body, LIMIT, (rows(share, length),) * 4, [smem()] + vmem(8),
        scratch=[pieces(share)],
    )(info, docs_front, q_front, *blocks_front, wo)
    sums = exchanged(partial_out[1:])
    forward_out = kernel(finish_front_body, 8, rows(share, length), vmem(5), 1.0)(
        partial_out[0], *sums, sent
    )

    d_parts = kernel(
        input_terms_body, LIMIT,
        jax.ShapeDtypeStruct((parts, share + 16, length), BF), vmem(9),
    )(d_query, t_own, back_two, back_four, q_back, kv_back, wk, wv, wq)
    d_parts = lax.all_to_all(d_parts, "fsdp", 0, 0)
    input_grad = kernel(finish_body, 8, rows(share, length), vmem(5), 1.0)(
        d_parts, stash, sent, own_gain, factor
    )
    return (forward_out.T[None], input_grad.T[None])


def solution(mesh):
    placed = (
        P("seq", "fsdp"),
        P("pipe", "seq", "fsdp"),
        P("pipe", "seq", "fsdp"),
        P("pipe", "seq", "fsdp"),
        P("seq", "fsdp"),
        P("pipe", None),
        P("pipe", None, "fsdp"),
        P("pipe", None, "fsdp"),
        P("pipe", None, "fsdp"),
        P("pipe", "fsdp", None),
        P("pipe", None),
        P("pipe", None),
    )
    return jax.shard_map(
        step,
        mesh=mesh,
        in_specs=placed,
        out_specs=(P("pipe", "seq", "fsdp"), P("pipe", "seq", "fsdp")),
        check_vma=False,
    )
```

```python
import jax
import jax.numpy as jnp
from jax import lax
from jax.experimental import pallas as pl
from jax.experimental.pallas import tpu as pltpu
from jax.sharding import PartitionSpec as P


HEAD = 128
WINDOW = 512
SCALE = HEAD ** (-0.5)
BF = jnp.bfloat16
F32 = jnp.float32
LIMIT = 14
SENDS = (0, 1, 3, 2)


def dot_nn(left, right):
    return lax.dot_general(left, right, (((1,), (0,)), ((), ())), preferred_element_type=F32)


def dot_nt(left, right):
    return lax.dot_general(left, right, (((1,), (1,)), ((), ())), preferred_element_type=F32)


def dot_tn(left, right):
    return lax.dot_general(left, right, (((0,), (0,)), ((), ())), preferred_element_type=F32)


def vmem(count):
    return [pl.BlockSpec(memory_space=pltpu.VMEM) for _ in range(count)]


def any_space():
    return pl.BlockSpec(memory_space=pl.ANY)


def smem():
    return pl.BlockSpec(memory_space=pltpu.SMEM)


def limit(mebibytes):
    return pltpu.CompilerParams(vmem_limit_bytes=mebibytes * 2**20)


def cost(microseconds):
    return pl.CostEstimate(
        flops=0, transcendentals=0, bytes_accessed=int(microseconds * 3_300_000)
    )


def kernel(body, mebibytes, out_shape, in_specs, microseconds=4.0, scratch=()):
    single = not isinstance(out_shape, tuple)
    return pl.pallas_call(
        body,
        out_shape=out_shape,
        in_specs=in_specs,
        out_specs=vmem(1)[0] if single else tuple(vmem(len(out_shape))),
        scratch_shapes=scratch,
        compiler_params=limit(mebibytes),
        cost_estimate=cost(microseconds),
    )


def stacked(ref, start, share):
    return jnp.concatenate([ref[part, start : start + share, :] for part in range(ref.shape[0])], 0)


def normal_rows(value, gain_ref):
    value = jnp.transpose(value).astype(F32)
    mean = jnp.mean(value * value, axis=1, keepdims=True)
    factor = lax.rsqrt(mean + 1e-06)
    return (value * factor * gain_ref[...]).astype(BF), factor


def across(column):
    length = column.shape[0]
    return jnp.transpose(jnp.broadcast_to(column, (length, length)))


def project_rows(h, wk_ref, wv_ref, wq_ref, q_ref, kv_ref):
    half = kv_ref.shape[1] // 2
    kv_ref[:, :half] = dot_nn(h, wk_ref[...]).astype(BF)
    kv_ref[:, half:] = dot_nn(h, wv_ref[...]).astype(BF)
    q_ref[...] = dot_nn(h, wq_ref[...]).astype(BF)


def placed_parts(info_ref, own, one, minus, far, hold_ref):
    place = info_ref[2]
    parts = hold_ref.shape[0]
    for offset, piece in ((0, own), (parts - 1, one), (1, minus), (2, far)):
        hold_ref[lax.rem(place + offset, parts)] = piece[...]


def spread_body(x_ref, out_ref, sems):
    copies = [
        pltpu.make_async_copy(x_ref, out_ref.at[part], sems.at[part])
        for part in range(out_ref.shape[0])
    ]
    for copy in copies:
        copy.start()
    for copy in copies:
        copy.wait()


def project_back_body(x_ref, gain_ref, wk_ref, wv_ref, wq_ref, q_ref, kv_ref, r_ref):
    h, factor = normal_rows(stacked(x_ref, 0, x_ref.shape[1]), gain_ref)
    r_ref[...] = jnp.broadcast_to(factor, r_ref.shape)
    project_rows(h, wk_ref, wv_ref, wq_ref, q_ref, kv_ref)


def project_front_body(
    info_ref, own, one, minus, far, gain_ref, wk_ref, wv_ref, wq_ref, wo_ref,
    q_ref, kv_ref, da_ref, hold_ref,
):
    placed_parts(info_ref, own, one, minus, far, hold_ref)
    share = hold_ref.shape[1] // 2
    h, _ = normal_rows(stacked(hold_ref, 0, share), gain_ref)
    project_rows(h, wk_ref, wv_ref, wq_ref, q_ref, kv_ref)
    grad = dot_nn(wo_ref[...], stacked(hold_ref, share, share))
    da_ref[...] = jnp.transpose(grad.astype(BF))


def touch_body(info_ref, gain_ref, out_ref, hold_ref):
    share, length = out_ref.shape
    hold_ref[...] = jnp.transpose(jnp.broadcast_to(gain_ref[...], (length, gain_ref.shape[1])))
    out_ref[...] = hold_ref[pl.ds(pl.multiple_of(info_ref[2] * share, 32), share), :]


def choose_body(info_ref, emb_ref, arr_ref, loss_ref, ret_ref, out_ref):
    share = emb_ref.shape[0]
    out_ref[:share] = jnp.where(info_ref[3] == 1, emb_ref[...], arr_ref[...])
    out_ref[share:] = jnp.where(info_ref[4] == 1, loss_ref[...], ret_ref[...])


def select_body(info_ref, kv_ref, four_ref, out_ref):
    out_ref[...] = jnp.where(info_ref[0] == 0, kv_ref[...], four_ref[...])


def combine_body(info_ref, own_ref, two_ref, four_ref, swap_ref, town_ref, ttwo_ref, tfour_ref):
    length = own_ref.shape[0]
    core = info_ref[0]
    late = swap_ref[:length].astype(F32)
    mid = swap_ref[length:].astype(F32)
    town_ref[...] = own_ref[...] + jnp.where(core == 0, mid, 0.0)
    ttwo_ref[...] = (two_ref[...] + late).astype(BF)
    tfour_ref[...] = (four_ref[...] + jnp.where(core == 0, 0.0, mid)).astype(BF)


def window_mask(info_ref, docs_ref, length):
    core = info_ref[0]
    index = info_ref[1]
    offsets = (0, 2, 4, 3 - 2 * core, 1 + 2 * core)
    q_row = jnp.broadcast_to(docs_ref[pl.ds(index, 1), :], (length, length))
    q_doc = jnp.transpose(q_row)
    across = lax.broadcasted_iota(jnp.int32, (length, length), 1)
    down = lax.broadcasted_iota(jnp.int32, (length, length), 0)
    masks = []
    for offset in offsets:
        block = index - offset
        k_doc = docs_ref[pl.ds(jnp.maximum(block, 0), 1), :]
        ahead = down - across + offset * length
        keep = (ahead >= 0) & (ahead < WINDOW) & (block >= 0)
        masks.append(keep & (jnp.broadcast_to(k_doc, (length, length)) == q_doc))
    return jnp.concatenate([jnp.where(m, 0.0, -1e30) for m in masks], axis=1)


def softmax_rows(q_rows, keys, bias):
    scores = dot_nt(q_rows, keys) * SCALE + bias
    top = jnp.max(scores, axis=1, keepdims=True)
    expo = jnp.exp(scores - top)
    return expo / jnp.sum(expo, axis=1, keepdims=True)


def head_rows(blocks, start):
    return jnp.concatenate([block[:, start : start + HEAD] for block in blocks], axis=0)


def attend_body(info_ref, docs_ref, q_ref, own, two, four, mid, late, wo_ref, out_ref):
    length = q_ref.shape[0]
    kv_heads = own.shape[1] // (2 * HEAD)
    groups = q_ref.shape[1] // HEAD // kv_heads
    bias = window_mask(info_ref, docs_ref, length)
    blocks = (own, two, four, mid, late)
    heads = []
    for kv in range(kv_heads):
        keys = head_rows(blocks, kv * HEAD)
        values = head_rows(blocks, (kv_heads + kv) * HEAD)
        for group in range(groups):
            head = kv * groups + group
            rows = q_ref[:, head * HEAD : (head + 1) * HEAD]
            probs = softmax_rows(rows, keys, bias).astype(BF)
            heads.append(dot_nn(probs, values).astype(BF))
    mixed = jnp.concatenate(heads, axis=1)
    whole = jnp.transpose(dot_nn(mixed, wo_ref[...]).astype(BF))
    out_ref[...] = whole.reshape(out_ref.shape)


def attend_back_body(
    info_ref, docs_ref, q_ref, da_ref, own, two, four, mid, late,
    dq_ref, town_ref, ttwo_ref, tfour_ref, tswap_ref,
):
    length = da_ref.shape[0]
    kv_heads = own.shape[1] // (2 * HEAD)
    groups = q_ref.shape[1] // HEAD // kv_heads
    bias = window_mask(info_ref, docs_ref, length)
    blocks = (own, two, four, mid, late)
    for kv in range(kv_heads):
        at = (kv_heads + kv) * HEAD
        keys = head_rows(blocks, kv * HEAD)
        values = head_rows(blocks, at)
        d_key = d_value = 0.0
        for group in range(groups):
            head = kv * groups + group
            span = slice(head * HEAD, (head + 1) * HEAD)
            rows = q_ref[:, span]
            grad = da_ref[:, span]
            probs = softmax_rows(rows, keys, bias)
            d_value = d_value + dot_tn(probs.astype(BF), grad)
            d_probs = dot_nt(grad, values)
            delta = jnp.sum(probs * d_probs, axis=1, keepdims=True)
            d_scores = (probs * (d_probs - delta)).astype(BF)
            dq_ref[:, span] = (dot_nn(d_scores, keys) * SCALE).astype(BF)
            d_key = d_key + dot_tn(d_scores, rows)
        for terms, start in ((d_key, kv * HEAD), (d_value, at)):
            cols = slice(start, start + HEAD)
            town_ref[:, cols] = terms[:length]
            ttwo_ref[:, cols] = terms[length : 2 * length]
            tfour_ref[:, cols] = terms[2 * length : 3 * length]
            tswap_ref[:length, cols] = terms[4 * length :].astype(BF)
            tswap_ref[length:, cols] = terms[3 * length : 4 * length].astype(BF)


def input_terms_body(
    dq_ref, own_ref, two_ref, four_ref, q_ref, kv_ref, front_ref, wk_ref, wv_ref, wq_ref, out_ref
):
    parts, rows, length = out_ref.shape
    share = wq_ref.shape[0] // parts
    out_ref[:, :share, :] = front_ref[...]
    half = own_ref.shape[1] // 2
    total = own_ref[...] + two_ref[...].astype(F32) + four_ref[...].astype(F32)
    d_key = (total[:, :half] * SCALE).astype(BF)
    d_value = total[:, half:].astype(BF)
    d_query = dq_ref[...]
    row = jnp.sum(q_ref[...].astype(F32) * d_query.astype(F32), axis=1, keepdims=True)
    keys = kv_ref[:, :half].astype(F32) * d_key.astype(F32)
    values = kv_ref[:, half:].astype(F32) * d_value.astype(F32)
    row = across(row + jnp.sum(keys + values, axis=1, keepdims=True))[: rows - 2 * share]
    high = row.astype(BF).astype(F32)
    first = lax.broadcasted_iota(jnp.int32, (rows - 2 * share, length), 0) == 0
    pair = jnp.where(first, high, row - high).astype(BF)
    for part in range(parts):
        span = slice(part * share, (part + 1) * share)
        d_norm = dot_nt(wq_ref[span], d_query)
        d_norm = d_norm + dot_nt(wk_ref[span], d_key)
        d_norm = d_norm + dot_nt(wv_ref[span], d_value)
        out_ref[part, share : 2 * share] = d_norm.astype(BF)
        out_ref[part, 2 * share :] = pair


def finish_body(sums_ref, x_ref, both_ref, gain_ref, r_ref, front_ref, back_ref):
    share = x_ref.shape[0]
    parts = sums_ref.shape[0]
    total = sum(sums_ref[part].astype(F32) for part in range(parts))
    front_ref[...] = (both_ref[:share].astype(F32) + total[:share]).astype(BF)
    last = 2 * share
    row = (total[last : last + 1] + total[last + 1 : last + 2]) / (parts * share)
    factor = jnp.transpose(r_ref[...])[:1]
    d_input = factor * gain_ref[...] * total[share:last]
    d_input = d_input - x_ref[...].astype(F32) * (factor * factor * row)
    back_ref[...] = (both_ref[share:].astype(F32) + d_input).astype(BF)


def shifted(value, steps):
    count = lax.axis_size("seq")
    pairs = [(s, s + steps) for s in range(count) if 0 <= s + steps < count]
    return lax.ppermute(value, "seq", pairs)


def swapped(value):
    count = lax.axis_size("seq")
    return lax.ppermute(value, "seq", [(s, s ^ 1) for s in range(count)])


def next_section(value, steps):
    count = lax.axis_size("pipe")
    pairs = [(s, s + steps) for s in range(count) if 0 <= s + steps < count]
    return lax.ppermute(value, "pipe", pairs)


def exchanged(values):
    count = lax.axis_size("fsdp")
    received = []
    for value, offset in zip(values, SENDS[1:]):
        pairs = [(s, (s + offset) % count) for s in range(count)]
        received.append(lax.ppermute(value, "fsdp", pairs))
    return received


def window_blocks(info, kv):
    two = shifted(kv, 2)
    four = shifted(kv, 4)
    mine = kernel(
        select_body, 4, jax.ShapeDtypeStruct(kv.shape, BF),
        [smem()] + vmem(2), 0.5,
    )(info, kv, four)
    mid = swapped(mine)
    late = swapped(two)
    return (kv, two, four, mid, late)


def step(
    embedded, sent_forward, stashed, sent_backward, loss_grad, norm_gain,
    w_query, w_key, value_projection, w_out, forward_docs, backward_docs,
):
    length, share = embedded.shape
    parts = lax.axis_size("fsdp")
    section = lax.axis_index("pipe")
    sections = lax.axis_size("pipe")
    index = lax.axis_index("seq")
    first = (section == 0).astype(jnp.int32)
    last = (section == sections - 1).astype(jnp.int32)
    info = jnp.stack([index % 2, index, lax.axis_index("fsdp"), first, last]).astype(jnp.int32)
    gain = norm_gain
    docs_front = forward_docs[0].reshape(-1, length)
    docs_back = backward_docs[0].reshape(-1, length)
    wq, wk, wv, wo = w_query[0], w_key[0], value_projection[0], w_out[0]
    q_cols = wq.shape[1]
    kv_cols = 2 * wk.shape[1]

    def rows(count, cols, kind=BF):
        return jax.ShapeDtypeStruct((count, cols), kind)

    def pieces(count):
        return pltpu.VMEM((parts, count, length), BF)

    stash, ahead, behind, info = lax.optimization_barrier(
        (stashed[0].T, sent_forward[0].T, sent_backward[0].T, info)
    )
    arrived = next_section(ahead, 1)
    returned = next_section(behind, -1)
    spread = pl.pallas_call(
        spread_body,
        out_shape=jax.ShapeDtypeStruct((parts, share, length), BF),
        in_specs=[any_space()], out_specs=any_space(),
        scratch_shapes=[pltpu.SemaphoreType.DMA((parts,))],
        name="spread", compiler_params=limit(4), cost_estimate=cost(1.0),
    )(stash)
    gathered = lax.all_to_all(spread, "fsdp", 0, 0)
    own_gain = kernel(
        touch_body, LIMIT, rows(share, length, F32), [smem()] + vmem(1),
        scratch=[pltpu.VMEM((parts * share, length), F32)],
    )(info, gain)

    q_back, kv_back, factor = kernel(
        project_back_body, LIMIT,
        (rows(length, q_cols), rows(length, kv_cols), rows(length, length, F32)),
        vmem(5),
    )(gathered, gain, wk, wv, wq)
    blocks_back = window_blocks(info, kv_back)

    sent = kernel(
        choose_body, LIMIT, rows(2 * share, length), [smem()] + vmem(4), 4.0,
    )(info, embedded.T, arrived, loss_grad.T, returned)
    both = exchanged((sent,) * 3)
    q_front, kv_front, d_attn = kernel(
        project_front_body, LIMIT,
        (rows(length, q_cols), rows(length, kv_cols), rows(length, q_cols)),
        [smem()] + vmem(9), scratch=[pieces(2 * share)],
    )(info, sent, *both, gain, wk, wv, wq, wo)
    blocks_front = window_blocks(info, kv_front)

    terms = rows(length, kv_cols, F32)
    d_query, t_own, t_two, t_four, t_swap = kernel(
        attend_back_body, LIMIT,
        (rows(length, q_cols), terms, terms, terms, rows(2 * length, kv_cols)),
        [smem()] + vmem(8),
    )(info, docs_back, q_back, d_attn, *blocks_back)
    t_swap = swapped(t_swap)
    t_own, send_two, send_four = kernel(
        combine_body, LIMIT, (terms, rows(length, kv_cols), rows(length, kv_cols)),
        [smem()] + vmem(4), 1.0,
    )(info, t_own, t_two, t_four, t_swap)
    back_two = shifted(send_two, -2)
    back_four = shifted(send_four, -4)

    partial_out = kernel(
        attend_body, LIMIT, jax.ShapeDtypeStruct((parts, share, length), BF),
        [smem()] + vmem(8),
    )(info, docs_front, q_front, *blocks_front, wo)
    partial_sums = kernel(
        input_terms_body, LIMIT,
        jax.ShapeDtypeStruct((parts, 2 * share + 16, length), BF), vmem(10),
    )(d_query, t_own, back_two, back_four, q_back, kv_back, partial_out, wk, wv, wq)
    partial_sums = lax.all_to_all(partial_sums, "fsdp", 0, 0)
    forward_out, input_grad = kernel(
        finish_body, 8, (rows(share, length), rows(share, length)), vmem(5), 1.0
    )(partial_sums, stash, sent, own_gain, factor)
    return (forward_out.T[None], input_grad.T[None])


def solution(mesh):
    placed = (
        P("seq", "fsdp"),
        P("pipe", "seq", "fsdp"),
        P("pipe", "seq", "fsdp"),
        P("pipe", "seq", "fsdp"),
        P("seq", "fsdp"),
        P("pipe", None),
        P("pipe", None, "fsdp"),
        P("pipe", None, "fsdp"),
        P("pipe", None, "fsdp"),
        P("pipe", "fsdp", None),
        P("pipe", None),
        P("pipe", None),
    )
    return jax.shard_map(
        step,
        mesh=mesh,
        in_specs=placed,
        out_specs=(P("pipe", "seq", "fsdp"), P("pipe", "seq", "fsdp")),
        check_vma=False,
    )
```
